256 devices in a mesh: tm: 16 (over z, core), mesh: 16 (over y, x).
Axes of the slice: x: 4, y: 4, z: 8, core: 2. Of those that a mesh axis runs over, the one named last changes fastest.
Arguments:
- diag_blocks: float32 [16, 2048, 128], P('tm', 'mesh'), may hold values from -5 to 10, as said below
- coupling: float32 [16, 2048, 128], P('tm', 'mesh'), may hold values from -4 to 1.2, as said below
- arrow_cols: float32 [16, 64, 2048], P('tm', None, 'mesh'), may hold values from -0.005800485 to 0.005800485
- rhs: float32 [16, 2048], P('tm', 'mesh'), may hold values from -3 to 3
- tip_rhs: float32 [64], replicated, may hold values from -6 to 6
- tip_diag: float32 [64], replicated, may hold values from 4 to 6
- config_shift: float32 [4], replicated, may hold values from 0.001 to 0.3
- config_coupling: float32 [4], replicated, may hold values from 0.99 to 1
- pattern: int32 [16, 16], P('tm', 'mesh'), may hold values 0 or 1
Outputs:
- log_diag: float32 [4, 16, 2048], P(None, 'tm', 'mesh')
- forward: float32 [4, 16, 2048], P(None, 'tm', 'mesh')
- tip_log: float32 [4, 64], replicated
- tip_forward: float32 [4, 64], replicated
The draws below stay inside these ranges and needn't reach their ends.
Inputs may be any that keep to these rules, and one draw needn't show every extreme that they name: Every tile of diag_blocks is symmetric, and for every setting in the stated ranges the block matrix with diagonal tiles A[t,i] + config_shift[c] I and coupling tiles B[c,t,i] is positive definite. Every tile of coupling is symmetric.
All inputs are finite; a program needn't handle non-finite values. No bound on the sum of `pattern` on one device may be relied on, other than what follows from the above.
Results may differ from the reference program's by a relative error of at most 0.0003.
Values sent between devices are 32-bit elements; how exact they have to be, the bound alone decides.
A program may use at most 128 MiB of HBM per device.

```python
import jax
import jax.numpy as jnp
from jax import lax

TILE = 128
TIP = 64
CONFIGS = 4
TIMES = 16
NTILES = 16
NODES = 2048


def coupling_weights(key):
    ntile = NODES // TILE
    raw = jax.random.truncated_normal(jax.random.fold_in(key, 7001), -5.0, 5.0, (TIMES + 1, ntile, TILE, TILE), jnp.float32)
    sym = (raw + jnp.swapaxes(raw, 2, 3)) * (0.35 / (2.0 * TILE) ** 0.5)
    level = 2.0
    return level * (sym + jnp.eye(TILE, dtype=jnp.float32))


def nugget_tiles(key):
    ntile = NODES // TILE
    basis, _ = jnp.linalg.qr(jax.random.normal(jax.random.fold_in(key, 7003), (ntile, TILE, TILE), jnp.float32))
    low_end = 0.0001
    base = jnp.exp(jax.random.uniform(jax.random.fold_in(key, 7004), (1, ntile, TILE), jnp.float32, jnp.log(low_end), 0.0))
    rough = jax.random.uniform(jax.random.fold_in(key, 7005), (TIMES, ntile, TILE), jnp.float32, 0.5, 2.0)
    levels = base * rough
    return jnp.einsum('nik,tnk,njk->tnij', basis, levels, basis)


def draw_diag_blocks(key, part):
    weights = coupling_weights(key)
    tiles = weights[:-1] + weights[1:] + nugget_tiles(key)
    return tiles.reshape(TIMES, NODES, TILE)


def draw_coupling(key, part):
    weights = coupling_weights(key)
    return (-weights[:-1]).reshape(TIMES, NODES, TILE)


def draw_config_shift(key, part):
    lowest = 0.001
    highest = 0.3
    middle = jnp.exp(jax.random.uniform(jax.random.fold_in(key, 7101), (CONFIGS - 2,), jnp.float32, jnp.log(lowest), jnp.log(highest)))
    values = jnp.concatenate([jnp.array([lowest, highest], jnp.float32), middle])
    shuffle = jax.random.permutation(jax.random.fold_in(key, 7102), CONFIGS)
    return values[shuffle]


def place_ends(values, key, least, largest):
    shape = values.shape
    place = [jax.random.randint(jax.random.fold_in(key, axis), (), 0, shape[axis]) for axis in range(len(shape))]
    values = values.at[tuple(place)].set(least)
    longest = shape.index(max(shape))
    place[longest] = (place[longest] + 1) % shape[longest]
    return values.at[tuple(place)].set(largest)


def block_levels(own_key, shape, shards, least, largest):
    def one(dim, shards_of):
        steps = jax.random.uniform(jax.random.fold_in(jax.random.fold_in(own_key, 6), dim), (shards_of,), jnp.float32, least / len(shards), largest / len(shards))
        return jnp.repeat(jnp.exp(steps), shape[dim] // shards_of).reshape((-1,) + (1,) * (len(shape) - dim - 1))

    level = one(*shards[0])
    for cut in shards[1:]:
        level = level * one(*cut)
    return level


def bell_draw(stream_key, shape, scale, limit, split=(), kind=jnp.bfloat16):
    values = scale * jax.random.normal(stream_key, shape, jnp.float32)
    if split:
        values = values * block_levels(stream_key, shape, split, -0.22, 0.18)
    return jnp.clip(values, -limit, limit).astype(kind)


def setup_inputs(seed: int = 0) -> dict:
    key_of = jax.random.split(jax.random.key(seed), 10)
    diag_blocks = draw_diag_blocks(jax.random.fold_in(key_of[9], 71), 0)
    coupling = draw_coupling(jax.random.fold_in(key_of[9], 71), 0)
    arrow_cols = bell_draw(key_of[2], (TIMES, TIP, NODES), (0.35 / (TIMES * NODES) ** 0.5), 0.005800485, ((0, 16), (2, 16)), jnp.float32)
    rhs = bell_draw(key_of[3], (TIMES, NODES), 0.5, 3.0, ((0, 16), (1, 16)), jnp.float32)
    tip_rhs = bell_draw(key_of[4], (TIP,), 1.0, 6.0, (), jnp.float32)
    tip_diag = jnp.clip(jax.random.uniform(key_of[5], (TIP,), jnp.float32, 4.0, 6.0), 4.0, 6.0)
    config_shift = draw_config_shift(jax.random.fold_in(key_of[9], 71), 0)
    config_coupling = jnp.clip(jax.random.uniform(key_of[7], (CONFIGS,), jnp.float32, 0.99, 1.0), 0.99, 1.0)
    pattern = place_ends((jax.random.randint(key_of[8], (TIMES, NTILES), 0, 64) < 63).astype(jnp.int32), jax.random.fold_in(key_of[8], 1), 0, 1)
    return {"diag_blocks": diag_blocks, "coupling": coupling, "arrow_cols": arrow_cols, "rhs": rhs, "tip_rhs": tip_rhs, "tip_diag": tip_diag, "config_shift": config_shift, "config_coupling": config_coupling, "pattern": pattern}


def lower_solve(low, right):
    return lax.linalg.triangular_solve(low, right, left_side=True, lower=True)

def block_step(prev, blocks, shift_value, couple_value):
    low_prev, arrow_prev, solved_prev = prev
    diag_tile, couple_tile, arrow_tile, right_tile, mask_tile, first = blocks
    high = lax.Precision.HIGHEST
    dtype = diag_tile.dtype
    eye = jnp.eye(diag_tile.shape[-1], dtype=dtype)
    low_prev = low_prev + (1.0 - first) * eye
    scaled = couple_tile * (couple_value * first * mask_tile.astype(dtype))[:, None, None]
    temp = lower_solve(low_prev, jnp.swapaxes(scaled, 1, 2))
    factor_c = jnp.swapaxes(temp, 1, 2)
    schur = diag_tile + shift_value * eye - jnp.einsum('nij,nkj->nik', factor_c, factor_c, precision=high)
    low = jnp.linalg.cholesky(schur)
    arrow = lower_solve(low, arrow_tile - jnp.einsum('nij,njk->nik', factor_c, arrow_prev, precision=high))
    inner = right_tile - jnp.einsum('nij,nj->ni', factor_c, solved_prev, precision=high)
    solved = lower_solve(low, inner[..., None])[..., 0]
    cross = jnp.einsum('nik,nil->kl', arrow, arrow, precision=high)
    cross_rhs = jnp.einsum('nik,ni->k', arrow, solved, precision=high)
    log_entries = jnp.log(jnp.diagonal(low, axis1=1, axis2=2))
    return ((low, arrow, solved), (log_entries, cross, cross_rhs))

def tip_solve(cross, cross_rhs, tip_rhs, tip_diag):
    precision_tip = jnp.diag(tip_diag) - cross
    low_tip = jnp.linalg.cholesky(precision_tip)
    solved = lower_solve(low_tip, (tip_rhs - cross_rhs)[:, None])[:, 0]
    return (jnp.log(jnp.diagonal(low_tip)), solved)

def reference(diag_blocks, coupling, arrow_cols, rhs, tip_rhs, tip_diag, config_shift, config_coupling, pattern):
    ntile = NODES // TILE
    dtype = diag_blocks.dtype
    diag_all = diag_blocks.reshape(TIMES, ntile, TILE, TILE)
    couple_all = coupling.reshape(TIMES, ntile, TILE, TILE)
    arrow_all = arrow_cols.reshape(TIMES, TIP, ntile, TILE).transpose(0, 2, 3, 1)
    right_all = rhs.reshape(TIMES, ntile, TILE)
    firsts = (jnp.arange(TIMES) > 0).astype(dtype)
    blocks = (diag_all, couple_all, arrow_all, right_all, pattern, firsts)

    def chain(shift_value, couple_value):

        def one(carry, xs):
            low_prev, arrow_prev, solved_prev, cross_sum, rhs_sum = carry
            new, (log_entries, cross, cross_rhs) = block_step((low_prev, arrow_prev, solved_prev), xs, shift_value, couple_value)
            return (new + (cross_sum + cross, rhs_sum + cross_rhs), (log_entries, new[2]))
        init = (jnp.zeros((ntile, TILE, TILE), dtype), jnp.zeros((ntile, TILE, TIP), dtype), jnp.zeros((ntile, TILE), dtype), jnp.zeros((TIP, TIP), dtype), jnp.zeros((TIP,), dtype))
        final, (logs, solved) = lax.scan(one, init, blocks)
        tip_log, tip_forward = tip_solve(final[3], final[4], tip_rhs, tip_diag)
        return (logs.reshape(TIMES, NODES), solved.reshape(TIMES, NODES), tip_log, tip_forward)
    log_diag, forward, tip_log, tip_forward = jax.vmap(chain)(config_shift, config_coupling)
    return (log_diag, forward, tip_log, tip_forward)
```

```python
import functools

import jax
import jax.numpy as jnp
from jax import lax
from jax.experimental import pallas as pl
from jax.experimental.pallas import tpu as pltpu
from jax.sharding import PartitionSpec as P

F32 = jnp.float32
GROUP = 4
HROWS = 72
MESH_ID = pl.DeviceIdType.MESH
VM = pltpu.VMEM
NT = (((1,), (1,)), ((), ()))


def vspec():
    return pl.BlockSpec(memory_space=pltpu.VMEM)


def sspec():
    return pl.BlockSpec(memory_space=pltpu.SMEM)


def dot_nt(a, b):
    return lax.dot_general(a, b, NT, precision=lax.Precision.HIGHEST, preferred_element_type=F32)


def lane_of(x, j):
    return jnp.broadcast_to(x[:, j : j + 1], x.shape)


def row_of(x, k):
    return jnp.broadcast_to(x[k : k + 1, :], x.shape)


def factor(mats, rows, width):
    tiles, wide = rows // 8, width // 8
    sub = lax.broadcasted_iota(jnp.int32, (8, 128), 0)
    lane = lax.broadcasted_iota(jnp.int32, (8, 128), 1)
    is_row = [sub == k for k in range(8)]
    mats = [list(m) for m in mats]
    pivots = [[None] * tiles for _ in mats]
    for base in range(0, rows, width):
        first = base // 8
        inside = (lane >= base) & (lane < base + width)
        state = []
        for mat in mats:
            panel = [mat[first + u] for u in range(wide)]
            cols = [[lane_of(panel[u], base + j) for u in range(wide)] for j in range(width)]
            panel = [
                jnp.where(inside, jnp.where(lane - base - 8 * u == sub, 1.0, 0.0), panel[u])
                for u in range(wide)
            ]
            state.append((panel, cols, list(panel), [jnp.ones((8, 128), F32)] * wide))
        for k in range(width):
            tile, row = divmod(k, 8)
            mine = is_row[row]
            for panel, cols, done, piv in state:
                pivot = row_of(cols[k][tile], row)
                inv = 1.0 / pivot
                kept = row_of(panel[tile], row)
                done[tile] = jnp.where(mine, kept, done[tile])
                piv[tile] = jnp.where(mine, pivot, piv[tile])
                kept = kept * inv
                own = cols[k]
                for u in range(wide):
                    new = panel[u] - own[u] * kept
                    panel[u] = jnp.where(mine, kept, new) if u == tile else new
                for j in range(k + 1, width):
                    mult = row_of(cols[j][tile], row) * inv
                    for u in range(wide):
                        new = cols[j][u] - own[u] * mult
                        cols[j][u] = jnp.where(mine, mult, new) if u == tile else new
        for (panel, cols, done, piv), mat, pivs in zip(state, mats, pivots):
            spread = [row_of(panel[j // 8], j % 8) for j in range(width)]
            for q in range(first + wide, tiles):
                old = mat[q]
                total = lane_of(old, base) * spread[0]
                for j in range(1, width):
                    total = total + lane_of(old, base + j) * spread[j]
                mat[q] = jnp.where(inside, 0.0, old) - total
            for u in range(wide):
                mat[first + u] = done[u]
                pivs[first + u] = piv[u]
    return mats, pivots


def inverse_factors(mats, width):
    sub = lax.broadcasted_iota(jnp.int32, (8, 128), 0)
    lane = lax.broadcasted_iota(jnp.int32, (8, 128), 1)
    tiled = [[m[8 * i : 8 * i + 8, :] for i in range(16)] for m in mats]
    done, pivots = factor(tiled, 128, width)
    inverses = [
        jnp.concatenate(
            [
                jnp.where(lane <= sub + 8 * i, d[i] * lax.rsqrt(p[i]), 0.0)
                for i in range(16)
            ],
            axis=0,
        )
        for d, p in zip(done, pivots)
    ]
    return inverses, pivots


def eye128():
    sub = lax.broadcasted_iota(jnp.int32, (128, 128), 0)
    lane = lax.broadcasted_iota(jnp.int32, (128, 128), 1)
    return jnp.where(sub == lane, 1.0, 0.0)


def eliminate(mats, stacks, width):
    inverses, _ = inverse_factors(mats, width)
    out = []
    for stack, inv in zip(stacks, inverses):
        half = dot_nt(stack, inv)
        out.append(dot_nt(half, half))
    return out


def gather_kernel(p_ref, out_ref, send, recv, own):
    me = lax.axis_index("tm")
    slot = lax.rem(me, GROUP)
    base = me - slot
    barrier = pltpu.get_barrier_semaphore()
    peers = [base + lax.rem(slot + d, GROUP) for d in range(1, GROUP)]
    for peer in peers:
        pl.semaphore_signal(barrier, inc=1, device_id={"tm": peer}, device_id_type=MESH_ID)
    local = pltpu.make_async_copy(p_ref, out_ref.at[slot], own)
    local.start()
    pl.semaphore_wait(barrier, GROUP - 1)
    copies = []
    for d, peer in enumerate(peers):
        copy = pltpu.make_async_remote_copy(
            src_ref=p_ref,
            dst_ref=out_ref.at[slot],
            send_sem=send.at[d],
            recv_sem=recv.at[d],
            device_id={"tm": peer},
            device_id_type=MESH_ID,
        )
        copy.start()
        copies.append(copy)
    local.wait()
    for copy in copies:
        copy.wait()


def group_gather(packed):
    return pl.pallas_call(
        gather_kernel,
        out_shape=jax.ShapeDtypeStruct((GROUP,) + packed.shape, F32),
        in_specs=[vspec()],
        out_specs=vspec(),
        scratch_shapes=[
            pltpu.SemaphoreType.DMA((GROUP - 1,)),
            pltpu.SemaphoreType.DMA((GROUP - 1,)),
            pltpu.SemaphoreType.DMA,
        ],
        compiler_params=pltpu.CompilerParams(collective_id=0, has_side_effects=True),
    )(packed)


def local_kernel(all_ref, shift_ref, couple_ref, d_ref, e_ref, u_ref, h_ref, g_ref, st_ref):
    slot = lax.rem(lax.axis_index("tm"), GROUP)
    shift, couple = shift_ref[slot], couple_ref[slot]
    eye = eye128()

    def diag(i):
        return all_ref[i, 0:128, :] + shift * eye

    def coup(i):
        return all_ref[i, 128:256, :] * couple

    def right(i):
        return all_ref[i, 256:328, :]

    m0 = jnp.concatenate([coup(1), coup(0), right(0)], axis=0)
    m2 = jnp.concatenate([coup(3), coup(2), right(2)], axis=0)
    ga, gb = eliminate([diag(0), diag(2)], [m0, m2], 8)
    d1 = diag(1) - ga[0:128, 0:128]
    et1 = -ga[128:256, 0:128]
    u1 = ga[128:256, 128:256]
    h1 = right(1) - ga[256:328, 0:128]
    g1 = -ga[256:328, 128:256]
    d_ref[0] = d1
    e_ref[0] = -ga[0:128, 128:256]
    u_ref[0] = u1
    h_ref[0] = h1
    g_ref[0] = g1
    db = diag(3) - gb[0:128, 0:128]
    eb = -gb[0:128, 128:256]
    ub = gb[128:256, 128:256]
    hb = right(3) - gb[256:328, 0:128]
    gvb = -gb[256:328, 128:256]
    n2 = jnp.concatenate([coup(2), et1, h1], axis=0)
    n3 = jnp.concatenate([eb, et1, h1 + gvb], axis=0)
    gc, gd = eliminate([d1, d1 - ub], [n2, n3], 8)
    d_ref[1] = diag(2) - gc[0:128, 0:128]
    e_ref[1] = -gc[0:128, 128:256]
    u_ref[1] = u1 + gc[128:256, 128:256]
    h_ref[1] = right(2) - gc[256:328, 0:128]
    g_ref[1] = g1 - gc[256:328, 128:256]
    d3 = db - gd[0:128, 0:128]
    h3 = hb - gd[256:328, 0:128]
    d_ref[2] = d3
    e_ref[2] = -gd[0:128, 128:256]
    u_ref[2] = u1 + gd[128:256, 128:256]
    h_ref[2] = h3
    g_ref[2] = g1 - gd[256:328, 128:256]
    st_ref[0:128, :] = d3
    st_ref[128:200, :] = h3


def local_phase(gathered, config_shift, config_coupling):
    tile = jax.ShapeDtypeStruct((3, 128, 128), F32)
    rows = jax.ShapeDtypeStruct((3, HROWS, 128), F32)
    return pl.pallas_call(
        local_kernel,
        out_shape=(tile, tile, tile, rows, rows, jax.ShapeDtypeStruct((200, 128), F32)),
        in_specs=[vspec(), sspec(), sspec()],
        out_specs=(vspec(),) * 6,
    )(gathered, config_shift, config_coupling)


def incoming(st_ref):
    seg = lax.axis_index("tm") // GROUP
    before = jnp.where(seg == 0, eye128(), st_ref[0:128, :])
    w = jnp.where(seg == 0, 0.0, st_ref[128:200, :])
    return before, w


def chain_kernel(st_ref, d_ref, e_ref, u_ref, h_ref, g_ref, out_ref):
    before, w = incoming(st_ref)
    stack = jnp.concatenate([e_ref[2], w + g_ref[2]], axis=0)
    (gram,) = eliminate([before - u_ref[2]], [stack], 16)
    out_ref[0:128, :] = d_ref[2] - gram[0:128, 0:128]
    out_ref[128:200, :] = h_ref[2] - gram[128:200, 0:128]


def chain_phase(state, parts):
    return pl.pallas_call(
        chain_kernel,
        out_shape=jax.ShapeDtypeStruct((200, 128), F32),
        in_specs=[vspec()] * 6,
        out_specs=vspec(),
    )(state, *parts)


def finish_kernel(
    chunks, st_ref, all_ref, shift_ref, couple_ref, d_ref, e_ref, u_ref, h_ref, g_ref,
    gram_ref, lf_ref, tip_ref,
):
    slot = lax.rem(lax.axis_index("tm"), GROUP)
    shift, couple = shift_ref[slot], couple_ref[slot]
    before, w = incoming(st_ref)
    sub = lax.broadcasted_iota(jnp.int32, (8, 128), 0)
    lane = lax.broadcasted_iota(jnp.int32, (8, 128), 1)
    mats = [before] + [before - u_ref[i] for i in range(3)]
    stacks = [jnp.concatenate([all_ref[0, 128:256, :] * couple, w], axis=0)] + [
        jnp.concatenate([e_ref[i], w + g_ref[i]], axis=0) for i in range(3)
    ]
    diags = [all_ref[0, 0:128, :] + shift * eye128()] + [d_ref[i] for i in range(3)]
    rights = [all_ref[0, 256:328, :]] + [h_ref[i] for i in range(3)]
    grams = eliminate(mats, stacks, 8)
    schur = [d - g[0:128, 0:128] for d, g in zip(diags, grams)]
    whole = [h - g[128:200, 0:128] for h, g in zip(rights, grams)]
    inverses, pivots = inverse_factors(schur, 8)
    total = None
    for i in range(GROUP):
        x = dot_nt(whole[i], inverses[i])
        gram = dot_nt(x, x)
        total = gram if total is None else total + gram
        logs = jnp.zeros((8, 128), F32)
        for k in range(16):
            logs = logs + jnp.where(lane == sub + 8 * k, jnp.log(pivots[i][k]), 0.0)
        lf_ref[i] = jnp.zeros((8, 128), F32)
        lf_ref[i, 0:1, :] = 0.5 * jnp.sum(logs, axis=0, keepdims=True)
        lf_ref[i, 1:2, :] = x[64:65, :]
    rows = 64 // chunks
    total = jnp.concatenate([total, jnp.zeros((HROWS, 128 - HROWS), F32)], axis=1)
    for m in range(chunks):
        gram_ref[m] = jnp.zeros((8, 128), F32)
        gram_ref[m, 0:rows, :] = total[rows * m : rows * (m + 1), :]
    tip_diag = all_ref[0, 321:322, :]
    tip_rhs = all_ref[0, 322:323, :]
    for i in range(8):
        on = lane == sub + 8 * i
        column = jnp.sum(jnp.where(on, tip_rhs, 0.0), axis=1, keepdims=True)
        tip_ref[8 * i : 8 * i + 8, :] = jnp.where(on, tip_diag, 0.0) + jnp.where(
            lane == 64, column, 0.0
        )


def finish_phase(state, gathered, config_shift, config_coupling, parts, chunks):
    return pl.pallas_call(
        functools.partial(finish_kernel, chunks),
        out_shape=(
            jax.ShapeDtypeStruct((chunks, 8, 128), F32),
            jax.ShapeDtypeStruct((GROUP, 8, 128), F32),
            jax.ShapeDtypeStruct((64, 128), F32),
        ),
        in_specs=[vspec()] * 2 + [sspec()] * 2 + [vspec()] * 5,
        out_specs=(vspec(),) * 3,
    )(state, gathered, config_shift, config_coupling, *parts)


def tail_kernel(
    chunks, segs, gram_ref, lf_ref, tip_ref, log_ref, fwd_ref, tlog_ref, tfwd_ref,
    lf_in, one_in, two_in, three_in, four_in, one_out, two_out, four_out,
    lf_s, lf_r, one_s, one_r, two_s, two_r, three_s, three_r, four_s, four_r,
):
    tm, me = lax.axis_index("tm"), lax.axis_index("mesh")
    slot = lax.rem(tm, GROUP)
    seg = tm // GROUP
    group = [seg * GROUP + lax.rem(slot + d, GROUP) for d in range(1, GROUP)]
    plane = [lax.rem(me + d, chunks) for d in range(1, chunks)]
    column = [slot + GROUP * lax.rem(seg + d, segs) for d in range(1, segs)]
    barrier = pltpu.get_barrier_semaphore()
    targets = [{"tm": t} for t in group] + [{"mesh": m} for m in plane] + [{"tm": t} for t in column]
    for target in targets:
        pl.semaphore_signal(barrier, inc=1, device_id=target, device_id_type=MESH_ID)
    pl.semaphore_wait(barrier, len(targets))

    def send(src, dst, ss, rs, target):
        copy = pltpu.make_async_remote_copy(
            src_ref=src, dst_ref=dst, send_sem=ss, recv_sem=rs, device_id=target, device_id_type=MESH_ID
        )
        copy.start()
        return copy

    one = [
        send(gram_ref.at[m], one_in.at[me], one_s.at[d], one_r.at[d], {"mesh": m})
        for d, m in enumerate(plane)
    ]
    lf = [
        send(lf_ref.at[lax.rem(slot + d + 1, GROUP)], lf_in.at[slot], lf_s.at[d], lf_r.at[d], {"tm": t})
        for d, t in enumerate(group)
    ]
    one_in[me] = gram_ref[me]
    lf_in[slot] = lf_ref[slot]
    for copy in one:
        copy.wait()
    total = one_in[0]
    for m in range(1, chunks):
        total = total + one_in[m]
    one_out[...] = total
    two_in[seg] = total
    two = [
        send(one_out, two_in.at[seg], two_s.at[d], two_r.at[d], {"tm": t})
        for d, t in enumerate(column)
    ]
    for copy in two:
        copy.wait()
    total = two_in[0]
    for m in range(1, segs):
        total = total + two_in[m]
    two_out[...] = total
    three_in[me] = total
    three = [
        send(two_out, three_in.at[me], three_s.at[d], three_r.at[d], {"mesh": m})
        for d, m in enumerate(plane)
    ]
    for copy in lf:
        copy.wait()
    for c in range(GROUP):
        log_ref[c : c + 1, :] = lf_in[c, 0:1, :]
        fwd_ref[c : c + 1, :] = lf_in[c, 1:2, :]
    for copy in three:
        copy.wait()
    rows = 64 // chunks
    summed = jnp.concatenate([three_in[m, 0:rows, :] for m in range(chunks)], axis=0)
    start = tip_ref[...] - summed
    ((done,), (pivots,)) = factor([[start[8 * i : 8 * i + 8, :] for i in range(8)]], 64, 16)
    sub = lax.broadcasted_iota(jnp.int32, (8, 128), 0)
    lane = lax.broadcasted_iota(jnp.int32, (8, 128), 1)
    logs = jnp.zeros((8, 128), F32)
    solved = jnp.zeros((8, 128), F32)
    for i in range(8):
        on = lane == sub + 8 * i
        logs = logs + jnp.where(on, jnp.log(pivots[i]), 0.0)
        solved = solved + jnp.where(on, lane_of(done[i], 64) * lax.rsqrt(pivots[i]), 0.0)
    result = jnp.where(
        sub == 0,
        0.5 * jnp.sum(logs, axis=0, keepdims=True),
        jnp.sum(solved, axis=0, keepdims=True),
    )
    four_out[...] = result
    four_in[slot] = result
    four = [
        send(four_out, four_in.at[slot], four_s.at[d], four_r.at[d], {"tm": t})
        for d, t in enumerate(group)
    ]
    for copy in four:
        copy.wait()
    for c in range(GROUP):
        tlog_ref[c : c + 1, :] = four_in[c, 0:1, 0:64]
        tfwd_ref[c : c + 1, :] = four_in[c, 1:2, 0:64]


def tail_phase(gram, lf, tip, chunks, segs):
    wide = jax.ShapeDtypeStruct((GROUP, 128), F32)
    narrow = jax.ShapeDtypeStruct((GROUP, 64), F32)
    dma = pltpu.SemaphoreType.DMA
    return pl.pallas_call(
        functools.partial(tail_kernel, chunks, segs),
        out_shape=(wide, wide, narrow, narrow),
        in_specs=[vspec()] * 3,
        out_specs=(vspec(),) * 4,
        scratch_shapes=[
            VM((GROUP, 8, 128), F32),
            VM((chunks, 8, 128), F32),
            VM((segs, 8, 128), F32),
            VM((chunks, 8, 128), F32),
            VM((GROUP, 8, 128), F32),
            VM((8, 128), F32),
            VM((8, 128), F32),
            VM((8, 128), F32),
            dma((GROUP - 1,)),
            dma((GROUP - 1,)),
            dma((chunks - 1,)),
            dma((chunks - 1,)),
            dma((segs - 1,)),
            dma((segs - 1,)),
            dma((chunks - 1,)),
            dma((chunks - 1,)),
            dma((GROUP - 1,)),
            dma((GROUP - 1,)),
        ],
        compiler_params=pltpu.CompilerParams(collective_id=1, has_side_effects=True),
    )(gram, lf, tip)


def shards(
    diag_blocks, coupling, arrow_cols, rhs, tip_rhs, tip_diag, config_shift, config_coupling, pattern
):
    groups, chunks = lax.axis_size("tm"), lax.axis_size("mesh")
    segs = groups // GROUP
    position = lax.axis_index("tm")
    keep = jnp.where(position > 0, pattern[0, 0], 0).astype(F32)
    wide = lambda v: jnp.concatenate([v, jnp.zeros((64,), F32)])[None]
    packed = jnp.concatenate(
        [
            diag_blocks[0],
            coupling[0] * keep,
            arrow_cols[0],
            rhs,
            wide(tip_diag),
            wide(tip_rhs),
            jnp.zeros((5, 128), F32),
        ],
        axis=0,
    )
    gathered = group_gather(packed)
    *parts, state = local_phase(gathered, config_shift, config_coupling)
    ring = [(s, s + GROUP) for s in range(groups - GROUP)]
    for r in range(segs - 1):
        state = lax.ppermute(state, "tm", ring)
        if r < segs - 2:
            state = chain_phase(state, parts)
    gram, lf, tip = finish_phase(state, gathered, config_shift, config_coupling, parts, chunks)
    log_diag, forward, tip_log, tip_forward = tail_phase(gram, lf, tip, chunks, segs)
    return (log_diag[:, None, :], forward[:, None, :], tip_log, tip_forward)


def solution(mesh):
    in_specs = (
        P("tm", "mesh", None),
        P("tm", "mesh", None),
        P("tm", None, "mesh"),
        P("tm", "mesh"),
        P(),
        P(),
        P(),
        P(),
        P("tm", "mesh"),
    )
    out_specs = (P(None, "tm", "mesh"), P(None, "tm", "mesh"), P(), P())
    return jax.shard_map(shards, mesh=mesh, in_specs=in_specs, out_specs=out_specs, check_vma=False)
```

```python
import functools

import jax
import jax.numpy as jnp
from jax import lax
from jax.experimental import pallas as pl
from jax.experimental.pallas import tpu as pltpu
from jax.sharding import PartitionSpec as P

F32 = jnp.float32
GROUP = 4
HROWS = 72
MESH_ID = pl.DeviceIdType.MESH
VM = pltpu.VMEM
NT = (((1,), (1,)), ((), ()))
NN = (((1,), (0,)), ((), ()))


def vspec():
    return pl.BlockSpec(memory_space=pltpu.VMEM)


def sspec():
    return pl.BlockSpec(memory_space=pltpu.SMEM)


def halves(x):
    high = x.astype(jnp.bfloat16)
    return high, (x - high.astype(F32)).astype(jnp.bfloat16)


def product(a, b, dims):
    ah, al = halves(a)
    bh, bl = halves(b)

    def one(x, y):
        return lax.dot_general(x, y, dims, preferred_element_type=F32)

    return one(ah, bh) + (one(ah, bl) + one(al, bh))


def dot_nt(a, b):
    return product(a, b, NT)


def lane_of(x, j):
    return jnp.broadcast_to(x[:, j : j + 1], x.shape)


def row_of(x, k):
    return jnp.broadcast_to(x[k : k + 1, :], x.shape)


def factor(mats, rows, width):
    tiles, wide = rows // 8, width // 8
    sub = lax.broadcasted_iota(jnp.int32, (8, 128), 0)
    lane = lax.broadcasted_iota(jnp.int32, (8, 128), 1)
    is_row = [sub == k for k in range(8)]
    mats = [list(m) for m in mats]
    pivots = [[None] * tiles for _ in mats]
    for base in range(0, rows, width):
        first = base // 8
        inside = (lane >= base) & (lane < base + width)
        state = []
        for mat in mats:
            panel = [mat[first + u] for u in range(wide)]
            cols = [[lane_of(panel[u], base + j) for u in range(wide)] for j in range(width)]
            panel = [
                jnp.where(inside, jnp.where(lane - base - 8 * u == sub, 1.0, 0.0), panel[u])
                for u in range(wide)
            ]
            ahead = None
            if first + wide < tiles:
                ahead = [
                    [lane_of(mat[first + wide + u], base + j) for j in range(width)]
                    for u in range(wide)
                ]
            state.append((panel, cols, list(panel), [jnp.ones((8, 128), F32)] * wide, ahead))
        for k in range(width):
            tile, row = divmod(k, 8)
            mine = is_row[row]
            for panel, cols, done, piv, _ in state:
                pivot = row_of(cols[k][tile], row)
                inv = 1.0 / pivot
                kept = row_of(panel[tile], row)
                done[tile] = jnp.where(mine, kept, done[tile])
                piv[tile] = jnp.where(mine, pivot, piv[tile])
                kept = kept * inv
                own = cols[k]
                for u in range(wide):
                    new = panel[u] - own[u] * kept
                    panel[u] = jnp.where(mine, kept, new) if u == tile else new
                for j in range(k + 1, width):
                    mult = row_of(cols[j][tile], row) * inv
                    for u in range(wide):
                        new = cols[j][u] - own[u] * mult
                        cols[j][u] = jnp.where(mine, mult, new) if u == tile else new
        for (panel, cols, done, piv, ahead), mat, pivs in zip(state, mats, pivots):
            start = first + wide
            if start < tiles:
                spread = [row_of(panel[j // 8], j % 8) for j in range(width)]
                for u in range(wide):
                    terms = [ahead[u][j] * spread[j] for j in range(width)]
                    while len(terms) > 1:
                        terms = [x + y for x, y in zip(terms[::2], terms[1::2])]
                    mat[start + u] = jnp.where(inside, 0.0, mat[start + u]) - terms[0]
                start += wide
            if start < tiles:
                zero = jnp.zeros((8, 128), F32)
                left = jnp.concatenate([jnp.where(inside, mat[q], 0.0) for q in range(start, tiles)], axis=0)
                right = jnp.concatenate([zero] * first + panel + [zero] * (16 - first - wide), axis=0)
                update = product(left, right, NN)
                for q in range(start, tiles):
                    row = 8 * (q - start)
                    mat[q] = jnp.where(inside, 0.0, mat[q]) - update[row : row + 8, :]
            for u in range(wide):
                mat[first + u] = done[u]
                pivs[first + u] = piv[u]
    return mats, pivots


def inverse_factors(mats, width):
    sub = lax.broadcasted_iota(jnp.int32, (8, 128), 0)
    lane = lax.broadcasted_iota(jnp.int32, (8, 128), 1)
    tiled = [[m[8 * i : 8 * i + 8, :] for i in range(16)] for m in mats]
    done, pivots = factor(tiled, 128, width)
    inverses = [
        jnp.concatenate(
            [
                jnp.where(lane <= sub + 8 * i, d[i] * lax.rsqrt(p[i]), 0.0)
                for i in range(16)
            ],
            axis=0,
        )
        for d, p in zip(done, pivots)
    ]
    return inverses, pivots


def eye128():
    sub = lax.broadcasted_iota(jnp.int32, (128, 128), 0)
    lane = lax.broadcasted_iota(jnp.int32, (128, 128), 1)
    return jnp.where(sub == lane, 1.0, 0.0)


def eliminate(mats, stacks, width):
    inverses, _ = inverse_factors(mats, width)
    out = []
    for stack, inv in zip(stacks, inverses):
        half = dot_nt(stack, inv)
        out.append(dot_nt(half, half[: half.shape[0] - HROWS]))
    return out


def gather_kernel(
    pat_ref, a_ref, c_ref, r_ref, y_ref, ao_ref, co_ref, ro_ref, xo_ref, x_ref,
    near_s, near_r, far_s, far_r, pass_s, pass_r, own,
):
    me = lax.axis_index("tm")
    slot = lax.rem(me, GROUP)
    base = me - slot
    core = lax.rem(slot, 2)
    far_slot = lax.rem(slot + 2, GROUP)
    near = {"tm": me + 1 - 2 * core}
    far = {"tm": base + far_slot}
    barrier = pltpu.get_barrier_semaphore()
    for peer in (near, far):
        pl.semaphore_signal(barrier, inc=1, device_id=peer, device_id_type=MESH_ID)
    x_ref[...] = jnp.zeros((8, 128), F32)
    x_ref[0:1, :] = y_ref[...]
    keep = jnp.where(me > 0, pat_ref[0, 0], 0).astype(F32)
    x_ref[1:2, :] = jnp.full((1, 128), 1.0, F32) * keep
    pl.semaphore_wait(barrier, 2)
    outs = (ao_ref, co_ref, ro_ref, xo_ref)
    mine = (a_ref.at[0], c_ref.at[0], r_ref.at[0], x_ref)

    def send(src, dst, ss, rs, target):
        copy = pltpu.make_async_remote_copy(
            src_ref=src, dst_ref=dst, send_sem=ss, recv_sem=rs, device_id=target, device_id_type=MESH_ID
        )
        copy.start()
        return copy

    far_copies = [
        send(mine[i], outs[i].at[slot], far_s.at[i], far_r.at[i], far) for i in range(4)
    ]
    near_copies = [
        send(mine[i], outs[i].at[slot], near_s.at[i], near_r.at[i], near) for i in range(4)
    ]
    local = [pltpu.make_async_copy(mine[i], outs[i].at[slot], own.at[i]) for i in range(4)]
    for copy in local:
        copy.start()
    passed = []
    for i in range(4):
        far_copies[i].wait_recv()
        passed.append(
            send(outs[i].at[far_slot], outs[i].at[far_slot], pass_s.at[i], pass_r.at[i], near)
        )
    for copy in local:
        copy.wait()
    for copy in far_copies:
        copy.wait_send()
    for copy in near_copies + passed:
        copy.wait()


def group_gather(pattern, diag_blocks, coupling, arrow_cols, rhs):
    dma = pltpu.SemaphoreType.DMA
    return pl.pallas_call(
        gather_kernel,
        out_shape=(
            jax.ShapeDtypeStruct((GROUP, 128, 128), F32),
            jax.ShapeDtypeStruct((GROUP, 128, 128), F32),
            jax.ShapeDtypeStruct((GROUP, 64, 128), F32),
            jax.ShapeDtypeStruct((GROUP, 8, 128), F32),
        ),
        in_specs=[sspec()] + [vspec()] * 4,
        out_specs=(vspec(),) * 4,
        scratch_shapes=[VM((8, 128), F32)] + [dma((4,))] * 7,
        compiler_params=pltpu.CompilerParams(collective_id=0, has_side_effects=True),
    )(pattern, diag_blocks, coupling, arrow_cols, rhs)


class Blocks:
    def __init__(self, a_ref, c_ref, r_ref, x_ref, shift_ref, couple_ref):
        slot = lax.rem(lax.axis_index("tm"), GROUP)
        self.refs = (a_ref, c_ref, r_ref, x_ref)
        self.shift, self.couple = shift_ref[slot], couple_ref[slot]

    def diag(self, i):
        return self.refs[0][i] + self.shift * eye128()

    def coup(self, i):
        return self.refs[1][i] * (self.refs[3][i, 1:2, :] * self.couple)

    def right(self, i):
        x = self.refs[3][i]
        sub = lax.broadcasted_iota(jnp.int32, (8, 128), 0)
        return jnp.concatenate([self.refs[2][i], jnp.where(sub == 0, x, 0.0)], axis=0)


def local_kernel(
    a_ref, c_ref, r_ref, x_ref, shift_ref, couple_ref, d_ref, e_ref, u_ref, h_ref, g_ref, st_ref, wt_ref
):
    blocks = Blocks(a_ref, c_ref, r_ref, x_ref, shift_ref, couple_ref)
    diag, coup, right = blocks.diag, blocks.coup, blocks.right
    m0 = jnp.concatenate([coup(1), coup(0), right(0)], axis=0)
    m2 = jnp.concatenate([coup(3), coup(2), right(2)], axis=0)
    ga, gb = eliminate([diag(0), diag(2)], [m0, m2], 8)
    d1 = diag(1) - ga[0:128, 0:128]
    et1 = -ga[128:256, 0:128]
    u1 = ga[128:256, 128:256]
    h1 = right(1) - ga[256:328, 0:128]
    g1 = -ga[256:328, 128:256]
    d_ref[0] = d1
    e_ref[0] = -ga[0:128, 128:256]
    u_ref[0] = u1
    h_ref[0] = h1
    g_ref[0] = g1
    db = diag(3) - gb[0:128, 0:128]
    eb = -gb[0:128, 128:256]
    ub = gb[128:256, 128:256]
    hb = right(3) - gb[256:328, 0:128]
    gvb = -gb[256:328, 128:256]
    n2 = jnp.concatenate([coup(2), et1, h1], axis=0)
    n3 = jnp.concatenate([eb, et1, h1 + gvb], axis=0)
    gc, gd = eliminate([d1, d1 - ub], [n2, n3], 8)
    d_ref[1] = diag(2) - gc[0:128, 0:128]
    e_ref[1] = -gc[0:128, 128:256]
    u_ref[1] = u1 + gc[128:256, 128:256]
    h_ref[1] = right(2) - gc[256:328, 0:128]
    g_ref[1] = g1 - gc[256:328, 128:256]
    d3 = db - gd[0:128, 0:128]
    h3 = hb - gd[256:328, 0:128]
    d_ref[2] = d3
    e_ref[2] = -gd[0:128, 128:256]
    u_ref[2] = u1 + gd[128:256, 128:256]
    h_ref[2] = h3
    g_ref[2] = g1 - gd[256:328, 128:256]
    st_ref[...] = d3
    wt_ref[...] = h3


def local_phase(gathered, config_shift, config_coupling):
    tile = jax.ShapeDtypeStruct((3, 128, 128), F32)
    rows = jax.ShapeDtypeStruct((3, HROWS, 128), F32)
    return pl.pallas_call(
        local_kernel,
        out_shape=(
            tile, tile, tile, rows, rows,
            jax.ShapeDtypeStruct((128, 128), F32),
            jax.ShapeDtypeStruct((HROWS, 128), F32),
        ),
        in_specs=[vspec()] * 4 + [sspec()] * 2,
        out_specs=(vspec(),) * 7,
    )(*gathered, config_shift, config_coupling)


def chain_kernel(
    segs, st_ref, wt_ref, d_ref, e_ref, u_ref, h_ref, g_ref, sin_ref, win_ref, s_out, w_out,
    send, recv,
):
    tm = lax.axis_index("tm")
    seg = tm // GROUP
    barrier = pltpu.get_barrier_semaphore()
    later = {"tm": tm + GROUP}
    earlier = {"tm": tm - GROUP}

    @pl.when(seg > 0)
    def _():
        pl.semaphore_signal(barrier, inc=1, device_id=earlier, device_id_type=MESH_ID)

    @pl.when(seg < segs - 1)
    def _():
        pl.semaphore_signal(barrier, inc=1, device_id=later, device_id_type=MESH_ID)

    pl.semaphore_wait(barrier, (seg > 0).astype(jnp.int32) + (seg < segs - 1).astype(jnp.int32))

    def copies(s_src, w_src):
        return [
            pltpu.make_async_remote_copy(
                src_ref=src, dst_ref=dst, send_sem=send.at[i], recv_sem=recv.at[i],
                device_id=later, device_id_type=MESH_ID,
            )
            for i, (src, dst) in enumerate([(s_src, sin_ref), (w_src, win_ref)])
        ]

    @pl.when(seg == 0)
    def _():
        out = copies(st_ref, wt_ref)
        for copy in out:
            copy.start()
        sin_ref[...] = eye128()
        win_ref[...] = jnp.zeros((HROWS, 128), F32)
        for copy in out:
            copy.wait_send()

    @pl.when(seg > 0)
    def _():
        out = copies(s_out, w_out)
        out[0].wait_recv()

        @pl.when(seg < segs - 1)
        def _():
            (inverse,), _ = inverse_factors([sin_ref[...] - u_ref[2]], 16)
            half = dot_nt(e_ref[2], inverse)
            s_out[...] = d_ref[2] - dot_nt(half, half)
            out[0].start()
            out[1].wait_recv()
            w_out[...] = h_ref[2] - dot_nt(dot_nt(win_ref[...] + g_ref[2], inverse), half)
            out[1].start()
            for copy in out:
                copy.wait_send()

        @pl.when(seg == segs - 1)
        def _():
            out[1].wait_recv()


def chain_phase(state, solved, parts, segs):
    tile = (128, 128)
    rows = (HROWS, 128)
    dma = pltpu.SemaphoreType.DMA
    return pl.pallas_call(
        functools.partial(chain_kernel, segs),
        out_shape=(jax.ShapeDtypeStruct(tile, F32), jax.ShapeDtypeStruct(rows, F32)),
        in_specs=[vspec()] * 7,
        out_specs=(vspec(),) * 2,
        scratch_shapes=[VM(tile, F32), VM(rows, F32), dma((2,)), dma((2,))],
        compiler_params=pltpu.CompilerParams(collective_id=1, has_side_effects=True),
    )(state, solved, *parts)


def finish_kernel(
    chunks, sin_ref, win_ref, a_ref, c_ref, r_ref, x_ref, shift_ref, couple_ref,
    d_ref, e_ref, u_ref, h_ref, g_ref, gram_ref, lf_ref,
):
    blocks = Blocks(a_ref, c_ref, r_ref, x_ref, shift_ref, couple_ref)
    before, w = sin_ref[...], win_ref[...]
    sub = lax.broadcasted_iota(jnp.int32, (8, 128), 0)
    lane = lax.broadcasted_iota(jnp.int32, (8, 128), 1)
    mats = [before] + [before - u_ref[i] for i in range(3)]
    stacks = [jnp.concatenate([blocks.coup(0), w], axis=0)] + [
        jnp.concatenate([e_ref[i], w + g_ref[i]], axis=0) for i in range(3)
    ]
    diags = [blocks.diag(0)] + [d_ref[i] for i in range(3)]
    rights = [blocks.right(0)] + [h_ref[i] for i in range(3)]
    grams = eliminate(mats, stacks, 8)
    schur = [d - g[0:128, 0:128] for d, g in zip(diags, grams)]
    whole = [h - g[128:200, 0:128] for h, g in zip(rights, grams)]
    inverses, pivots = inverse_factors(schur, 8)
    total = None
    for i in range(GROUP):
        x = dot_nt(whole[i], inverses[i])
        gram = dot_nt(x, x)
        total = gram if total is None else total + gram
        logs = jnp.zeros((8, 128), F32)
        for k in range(16):
            logs = logs + jnp.where(lane == sub + 8 * k, jnp.log(pivots[i][k]), 0.0)
        lf_ref[i] = jnp.zeros((8, 128), F32)
        lf_ref[i, 0:1, :] = 0.5 * jnp.sum(logs, axis=0, keepdims=True)
        lf_ref[i, 1:2, :] = x[64:65, :]
    rows = 64 // chunks
    total = jnp.concatenate([total, jnp.zeros((HROWS, 128 - HROWS), F32)], axis=1)
    for m in range(chunks):
        gram_ref[m] = jnp.zeros((8, 128), F32)
        gram_ref[m, 0:rows, :] = total[rows * m : rows * (m + 1), :]


def finish_phase(sin, win, gathered, config_shift, config_coupling, parts, chunks):
    return pl.pallas_call(
        functools.partial(finish_kernel, chunks),
        out_shape=(
            jax.ShapeDtypeStruct((chunks, 8, 128), F32),
            jax.ShapeDtypeStruct((GROUP, 8, 128), F32),
        ),
        in_specs=[vspec()] * 6 + [sspec()] * 2 + [vspec()] * 5,
        out_specs=(vspec(),) * 2,
    )(sin, win, *gathered, config_shift, config_coupling, *parts)


def tail_kernel(
    chunks, times, gram_ref, lf_ref, lf_in, three_in, one_in, two_in, one_out, two_out,
    lf_s, lf_r, one_s, one_r, two_s, two_r, three_s, three_r,
):
    tm, me = lax.axis_index("tm"), lax.axis_index("mesh")
    slot = lax.rem(tm, GROUP)
    group = [tm - slot + lax.rem(slot + d, GROUP) for d in range(1, GROUP)]
    plane = [lax.rem(me + d, chunks) for d in range(1, chunks)]
    column = [lax.rem(tm + d, times) for d in range(1, times)]
    barrier = pltpu.get_barrier_semaphore()
    targets = [{"mesh": m} for m in plane] + [{"tm": t} for t in column]
    for target in targets:
        pl.semaphore_signal(barrier, inc=1, device_id=target, device_id_type=MESH_ID)
    pl.semaphore_wait(barrier, len(targets))

    def send(src, dst, ss, rs, target):
        copy = pltpu.make_async_remote_copy(
            src_ref=src, dst_ref=dst, send_sem=ss, recv_sem=rs, device_id=target, device_id_type=MESH_ID
        )
        copy.start()
        return copy

    one = [
        send(gram_ref.at[m], one_in.at[me], one_s.at[d], one_r.at[d], {"mesh": m})
        for d, m in enumerate(plane)
    ]
    one_in[me] = gram_ref[me]
    for copy in one:
        copy.wait()
    total = one_in[0]
    for m in range(1, chunks):
        total = total + one_in[m]
    one_out[...] = total
    two_in[tm] = total
    two = [
        send(one_out, two_in.at[tm], two_s.at[d], two_r.at[d], {"tm": t})
        for d, t in enumerate(column)
    ]
    lf = [
        send(lf_ref.at[lax.rem(slot + d + 1, GROUP)], lf_in.at[slot], lf_s.at[d], lf_r.at[d], {"tm": t})
        for d, t in enumerate(group)
    ]
    lf_in[slot] = lf_ref[slot]
    for copy in two:
        copy.wait()
    rows = 64 // chunks
    for c in range(GROUP):
        total = two_in[c]
        for t in range(c + GROUP, times, GROUP):
            total = total + two_in[t]
        two_out[rows * c : rows * (c + 1), :] = total[0:rows, :]
    three = [
        send(two_out, three_in.at[me], three_s.at[d], three_r.at[d], {"mesh": m})
        for d, m in enumerate(plane)
    ]
    three_in[me] = two_out[...]
    for copy in lf + three:
        copy.wait()


def tail_phase(gram, lf, chunks, times):
    dma = pltpu.SemaphoreType.DMA
    rows = GROUP * 64 // chunks
    return pl.pallas_call(
        functools.partial(tail_kernel, chunks, times),
        out_shape=(
            jax.ShapeDtypeStruct((GROUP, 8, 128), F32),
            jax.ShapeDtypeStruct((chunks, rows, 128), F32),
        ),
        in_specs=[vspec()] * 2,
        out_specs=(vspec(),) * 2,
        scratch_shapes=[
            VM((chunks, 8, 128), F32),
            VM((times, 8, 128), F32),
            VM((8, 128), F32),
            VM((rows, 128), F32),
            dma((GROUP - 1,)),
            dma((GROUP - 1,)),
            dma((chunks - 1,)),
            dma((chunks - 1,)),
            dma((times - 1,)),
            dma((times - 1,)),
            dma((chunks - 1,)),
            dma((chunks - 1,)),
        ],
        compiler_params=pltpu.CompilerParams(collective_id=2, has_side_effects=True),
    )(gram, lf)


def tip_kernel(chunks, lf_ref, sum_ref, diag_ref, rhs_ref, log_ref, fwd_ref, tlog_ref, tfwd_ref):
    sub = lax.broadcasted_iota(jnp.int32, (8, 128), 0)
    lane = lax.broadcasted_iota(jnp.int32, (8, 128), 1)
    pad = jnp.zeros((1, 64), F32)
    diag = jnp.concatenate([diag_ref[...], pad], axis=1)
    rhs = jnp.concatenate([rhs_ref[...], pad], axis=1)
    rows = 64 // chunks
    start = []
    for i in range(8):
        on = lane == sub + 8 * i
        column = jnp.sum(jnp.where(on, rhs, 0.0), axis=1, keepdims=True)
        start.append(jnp.where(on, diag, 0.0) + jnp.where(lane == 64, column, 0.0))
    mats = []
    for c in range(GROUP):
        log_ref[c] = lf_ref[c, 0:1, :]
        fwd_ref[c] = lf_ref[c, 1:2, :]
        whole = jnp.concatenate(
            [sum_ref[m, rows * c : rows * (c + 1), :] for m in range(chunks)], axis=0
        )
        mats.append([start[i] - whole[8 * i : 8 * i + 8, :] for i in range(8)])
    done, pivots = factor(mats, 64, 8)
    for c in range(GROUP):
        logs = jnp.zeros((8, 128), F32)
        solved = jnp.zeros((8, 128), F32)
        for i in range(8):
            on = lane == sub + 8 * i
            logs = logs + jnp.where(on, jnp.log(pivots[c][i]), 0.0)
            solved = solved + jnp.where(on, lane_of(done[c][i], 64) * lax.rsqrt(pivots[c][i]), 0.0)
        tlog_ref[c : c + 1, :] = 0.5 * jnp.sum(logs, axis=0, keepdims=True)[:, 0:64]
        tfwd_ref[c : c + 1, :] = jnp.sum(solved, axis=0, keepdims=True)[:, 0:64]


def tip_phase(lf, summed, tip_diag, tip_rhs, chunks):
    wide = jax.ShapeDtypeStruct((GROUP, 1, 128), F32)
    narrow = jax.ShapeDtypeStruct((GROUP, 64), F32)
    return pl.pallas_call(
        functools.partial(tip_kernel, chunks),
        out_shape=(wide, wide, narrow, narrow),
        in_specs=[vspec()] * 4,
        out_specs=(vspec(),) * 4,
    )(lf, summed, tip_diag[None], tip_rhs[None])


def shards(
    diag_blocks, coupling, arrow_cols, rhs, tip_rhs, tip_diag, config_shift, config_coupling, pattern
):
    times, chunks = lax.axis_size("tm"), lax.axis_size("mesh")
    gathered = group_gather(pattern, diag_blocks, coupling, arrow_cols, rhs)
    *parts, state, solved = local_phase(gathered, config_shift, config_coupling)
    sin, win = chain_phase(state, solved, parts, times // GROUP)
    gram, lf = finish_phase(sin, win, gathered, config_shift, config_coupling, parts, chunks)
    lf, summed = tail_phase(gram, lf, chunks, times)
    return tip_phase(lf, summed, tip_diag, tip_rhs, chunks)


def solution(mesh):
    in_specs = (
        P("tm", "mesh", None),
        P("tm", "mesh", None),
        P("tm", None, "mesh"),
        P("tm", "mesh"),
        P(),
        P(),
        P(),
        P(),
        P("tm", "mesh"),
    )
    out_specs = (P(None, "tm", "mesh"), P(None, "tm", "mesh"), P(), P())
    return jax.shard_map(shards, mesh=mesh, in_specs=in_specs, out_specs=out_specs, check_vma=False)
```

```python
import functools

import jax
import jax.numpy as jnp
from jax import lax
from jax.experimental import pallas as pl
from jax.experimental.pallas import tpu as pltpu
from jax.sharding import PartitionSpec as P

F32 = jnp.float32
GROUP = 4
HROWS = 72
MESH_ID = pl.DeviceIdType.MESH
VM = pltpu.VMEM
NT = (((1,), (1,)), ((), ()))
NN = (((1,), (0,)), ((), ()))


def vspec():
    return pl.BlockSpec(memory_space=pltpu.VMEM)


def sspec():
    return pl.BlockSpec(memory_space=pltpu.SMEM)


def halves(x):
    high = x.astype(jnp.bfloat16)
    return high, (x - high.astype(F32)).astype(jnp.bfloat16)


def product(a, b, dims):
    ah, al = halves(a)
    bh, bl = halves(b)

    def one(x, y):
        return lax.dot_general(x, y, dims, preferred_element_type=F32)

    return one(ah, bh) + (one(ah, bl) + one(al, bh))


def dot_nt(a, b):
    return product(a, b, NT)


def lane_of(x, j):
    return jnp.broadcast_to(x[:, j : j + 1], x.shape)


def row_of(x, k):
    return jnp.broadcast_to(x[k : k + 1, :], x.shape)


def factor(mats, rows, width):
    tiles, wide = rows // 8, width // 8
    sub = lax.broadcasted_iota(jnp.int32, (8, 128), 0)
    lane = lax.broadcasted_iota(jnp.int32, (8, 128), 1)
    is_row = [sub == k for k in range(8)]
    mats = [list(m) for m in mats]
    pivots = [[None] * tiles for _ in mats]
    for base in range(0, rows, width):
        first = base // 8
        inside = (lane >= base) & (lane < base + width)
        state = []
        for mat in mats:
            panel = [mat[first + u] for u in range(wide)]
            cols = [[lane_of(panel[u], base + j) for u in range(wide)] for j in range(width)]
            panel = [
                jnp.where(inside, jnp.where(lane - base - 8 * u == sub, 1.0, 0.0), panel[u])
                for u in range(wide)
            ]
            ahead = None
            if first + wide < tiles:
                ahead = [
                    [lane_of(mat[first + wide + u], base + j) for j in range(width)]
                    for u in range(wide)
                ]
            state.append((panel, cols, list(panel), [jnp.ones((8, 128), F32)] * wide, ahead))
        for k in range(width):
            tile, row = divmod(k, 8)
            mine = is_row[row]
            for panel, cols, done, piv, _ in state:
                pivot = row_of(cols[k][tile], row)
                inv = 1.0 / pivot
                kept = row_of(panel[tile], row)
                done[tile] = jnp.where(mine, kept, done[tile])
                piv[tile] = jnp.where(mine, pivot, piv[tile])
                kept = kept * inv
                own = cols[k]
                for u in range(wide):
                    new = panel[u] - own[u] * kept
                    panel[u] = jnp.where(mine, kept, new) if u == tile else new
                for j in range(k + 1, width):
                    mult = row_of(cols[j][tile], row) * inv
                    for u in range(wide):
                        new = cols[j][u] - own[u] * mult
                        cols[j][u] = jnp.where(mine, mult, new) if u == tile else new
        for (panel, cols, done, piv, ahead), mat, pivs in zip(state, mats, pivots):
            start = first + wide
            if start < tiles:
                spread = [row_of(panel[j // 8], j % 8) for j in range(width)]
                for u in range(wide):
                    terms = [ahead[u][j] * spread[j] for j in range(width)]
                    while len(terms) > 1:
                        terms = [x + y for x, y in zip(terms[::2], terms[1::2])]
                    mat[start + u] = jnp.where(inside, 0.0, mat[start + u]) - terms[0]
                start += wide
            if start < tiles:
                zero = jnp.zeros((8, 128), F32)
                left = jnp.concatenate([jnp.where(inside, mat[q], 0.0) for q in range(start, tiles)], axis=0)
                right = jnp.concatenate([zero] * first + panel + [zero] * (16 - first - wide), axis=0)
                update = product(left, right, NN)
                for q in range(start, tiles):
                    row = 8 * (q - start)
                    mat[q] = jnp.where(inside, 0.0, mat[q]) - update[row : row + 8, :]
            for u in range(wide):
                mat[first + u] = done[u]
                pivs[first + u] = piv[u]
    return mats, pivots


def inverse_factors(mats, width):
    sub = lax.broadcasted_iota(jnp.int32, (8, 128), 0)
    lane = lax.broadcasted_iota(jnp.int32, (8, 128), 1)
    tiled = [[m[8 * i : 8 * i + 8, :] for i in range(16)] for m in mats]
    done, pivots = factor(tiled, 128, width)
    inverses = [
        jnp.concatenate(
            [
                jnp.where(lane <= sub + 8 * i, d[i] * lax.rsqrt(p[i]), 0.0)
                for i in range(16)
            ],
            axis=0,
        )
        for d, p in zip(done, pivots)
    ]
    return inverses, pivots


def eye128():
    sub = lax.broadcasted_iota(jnp.int32, (128, 128), 0)
    lane = lax.broadcasted_iota(jnp.int32, (128, 128), 1)
    return jnp.where(sub == lane, 1.0, 0.0)


def eliminate(mats, stacks, width):
    inverses, _ = inverse_factors(mats, width)
    out = []
    for stack, inv in zip(stacks, inverses):
        half = dot_nt(stack, inv)
        out.append(dot_nt(half, half[: half.shape[0] - HROWS]))
    return out


def gather_kernel(
    pat_ref, a_ref, c_ref, r_ref, y_ref, ao_ref, co_ref, ro_ref, xo_ref, x_ref,
    near_s, near_r, far_s, far_r, pass_s, pass_r, own,
):
    me = lax.axis_index("tm")
    slot = lax.rem(me, GROUP)
    base = me - slot
    core = lax.rem(slot, 2)
    far_slot = lax.rem(slot + 2, GROUP)
    near = {"tm": me + 1 - 2 * core}
    far = {"tm": base + far_slot}
    barrier = pltpu.get_barrier_semaphore()
    for peer in (near, far):
        pl.semaphore_signal(barrier, inc=1, device_id=peer, device_id_type=MESH_ID)
    x_ref[...] = jnp.zeros((8, 128), F32)
    x_ref[0:1, :] = y_ref[...]
    keep = jnp.where(me > 0, pat_ref[0, 0], 0).astype(F32)
    x_ref[1:2, :] = jnp.full((1, 128), 1.0, F32) * keep
    pl.semaphore_wait(barrier, 2)
    outs = (ao_ref, co_ref, ro_ref, xo_ref)
    mine = (a_ref.at[0], c_ref.at[0], r_ref.at[0], x_ref)

    def send(src, dst, ss, rs, target):
        copy = pltpu.make_async_remote_copy(
            src_ref=src, dst_ref=dst, send_sem=ss, recv_sem=rs, device_id=target, device_id_type=MESH_ID
        )
        copy.start()
        return copy

    far_copies = [
        send(mine[i], outs[i].at[slot], far_s.at[i], far_r.at[i], far) for i in range(4)
    ]
    near_copies = [
        send(mine[i], outs[i].at[slot], near_s.at[i], near_r.at[i], near) for i in range(4)
    ]
    local = [pltpu.make_async_copy(mine[i], outs[i].at[slot], own.at[i]) for i in range(4)]
    for copy in local:
        copy.start()
    passed = []
    for i in range(4):
        far_copies[i].wait_recv()
        passed.append(
            send(outs[i].at[far_slot], outs[i].at[far_slot], pass_s.at[i], pass_r.at[i], near)
        )
    for copy in local:
        copy.wait()
    for copy in far_copies:
        copy.wait_send()
    for copy in near_copies + passed:
        copy.wait()


def group_gather(pattern, diag_blocks, coupling, arrow_cols, rhs):
    dma = pltpu.SemaphoreType.DMA
    return pl.pallas_call(
        gather_kernel,
        out_shape=(
            jax.ShapeDtypeStruct((GROUP, 128, 128), F32),
            jax.ShapeDtypeStruct((GROUP, 128, 128), F32),
            jax.ShapeDtypeStruct((GROUP, 64, 128), F32),
            jax.ShapeDtypeStruct((GROUP, 8, 128), F32),
        ),
        in_specs=[sspec()] + [vspec()] * 4,
        out_specs=(vspec(),) * 4,
        scratch_shapes=[VM((8, 128), F32)] + [dma((4,))] * 7,
        compiler_params=pltpu.CompilerParams(collective_id=0, has_side_effects=True),
    )(pattern, diag_blocks, coupling, arrow_cols, rhs)


class Blocks:
    def __init__(self, a_ref, c_ref, r_ref, x_ref, shift_ref, couple_ref):
        slot = lax.rem(lax.axis_index("tm"), GROUP)
        self.refs = (a_ref, c_ref, r_ref, x_ref)
        self.shift, self.couple = shift_ref[slot], couple_ref[slot]

    def diag(self, i):
        return self.refs[0][i] + self.shift * eye128()

    def coup(self, i):
        return self.refs[1][i] * (self.refs[3][i, 1:2, :] * self.couple)

    def right(self, i):
        x = self.refs[3][i]
        sub = lax.broadcasted_iota(jnp.int32, (8, 128), 0)
        return jnp.concatenate([self.refs[2][i], jnp.where(sub == 0, x, 0.0)], axis=0)


def local_blocks(blocks, d_ref, e_ref, u_ref, h_ref, g_ref):
    diag, coup, right = blocks.diag, blocks.coup, blocks.right
    m0 = jnp.concatenate([coup(1), coup(0), right(0)], axis=0)
    m2 = jnp.concatenate([coup(3), coup(2), right(2)], axis=0)
    ga, gb = eliminate([diag(0), diag(2)], [m0, m2], 8)
    d1 = diag(1) - ga[0:128, 0:128]
    et1 = -ga[128:256, 0:128]
    u1 = ga[128:256, 128:256]
    h1 = right(1) - ga[256:328, 0:128]
    g1 = -ga[256:328, 128:256]
    d_ref[0] = d1
    e_ref[0] = -ga[0:128, 128:256]
    u_ref[0] = u1
    h_ref[0] = h1
    g_ref[0] = g1
    db = diag(3) - gb[0:128, 0:128]
    eb = -gb[0:128, 128:256]
    ub = gb[128:256, 128:256]
    hb = right(3) - gb[256:328, 0:128]
    gvb = -gb[256:328, 128:256]
    n2 = jnp.concatenate([coup(2), et1, h1], axis=0)
    n3 = jnp.concatenate([eb, et1, h1 + gvb], axis=0)
    gc, gd = eliminate([d1, d1 - ub], [n2, n3], 8)
    d_ref[2] = db - gd[0:128, 0:128]
    e_ref[2] = -gd[0:128, 128:256]
    u_ref[2] = u1 + gd[128:256, 128:256]
    h_ref[2] = hb - gd[256:328, 0:128]
    g_ref[2] = g1 - gd[256:328, 128:256]
    d_ref[1] = diag(2) - gc[0:128, 0:128]
    e_ref[1] = -gc[0:128, 128:256]
    u_ref[1] = u1 + gc[128:256, 128:256]
    h_ref[1] = right(2) - gc[256:328, 0:128]
    g_ref[1] = g1 - gc[256:328, 128:256]


def start_copy(src, dst, ss, rs, target):
    copy = pltpu.make_async_remote_copy(
        src_ref=src, dst_ref=dst, send_sem=ss, recv_sem=rs, device_id=target, device_id_type=MESH_ID
    )
    copy.start()
    return copy


def finish_blocks(chunks, blocks, sin_ref, win_ref, wait_w, d_ref, e_ref, u_ref, h_ref, g_ref, gram_ref, lf_ref):
    sub = lax.broadcasted_iota(jnp.int32, (8, 128), 0)
    lane = lax.broadcasted_iota(jnp.int32, (8, 128), 1)
    before = sin_ref[...]
    inverses, _ = inverse_factors([before] + [before - u_ref[i] for i in range(3)], 8)
    wait_w()
    w = win_ref[...]
    stacks = [jnp.concatenate([blocks.coup(0), w], axis=0)] + [
        jnp.concatenate([e_ref[i], w + g_ref[i]], axis=0) for i in range(3)
    ]
    diags = [blocks.diag(0)] + [d_ref[i] for i in range(3)]
    rights = [blocks.right(0)] + [h_ref[i] for i in range(3)]
    schur, whole = [], []
    for stack, inv, d, h in zip(stacks, inverses, diags, rights):
        half = dot_nt(stack, inv)
        gram = dot_nt(half, half[0:128])
        schur.append(d - gram[0:128])
        whole.append(h - gram[128:200])
    inverses, pivots = inverse_factors(schur, 8)
    total = None
    for i in range(GROUP):
        x = dot_nt(whole[i], inverses[i])
        gram = dot_nt(x, x)
        total = gram if total is None else total + gram
        logs = jnp.zeros((8, 128), F32)
        for k in range(16):
            logs = logs + jnp.where(lane == sub + 8 * k, jnp.log(pivots[i][k]), 0.0)
        lf_ref[i] = jnp.where(
            sub == 0,
            0.5 * jnp.sum(logs, axis=0, keepdims=True),
            jnp.where(sub == 1, x[64:65, :], 0.0),
        )
    rows = 64 // chunks
    total = jnp.concatenate([total, jnp.zeros((HROWS, 128 - HROWS), F32)], axis=1)
    for m in range(chunks):
        gram_ref[m] = jnp.concatenate(
            [total[rows * m : rows * (m + 1), :], jnp.zeros((8 - rows, 128), F32)], axis=0
        )


def main_kernel(
    chunks, times, a_ref, c_ref, r_ref, x_ref, shift_ref, couple_ref, lf_in, three_in,
    d_ref, e_ref, u_ref, h_ref, g_ref, sin_ref, win_ref, s_out, w_out, gram_ref, lf_ref,
    one_in, two_in, one_out, two_out, send, recv,
    lf_s, lf_r, one_s, one_r, two_s, two_r, three_s, three_r,
):
    tm, me = lax.axis_index("tm"), lax.axis_index("mesh")
    slot = lax.rem(tm, GROUP)
    seg = tm // GROUP
    segs = times // GROUP
    group = [tm - slot + lax.rem(slot + d, GROUP) for d in range(1, GROUP)]
    plane = [lax.rem(me + d, chunks) for d in range(1, chunks)]
    column = [lax.rem(tm + d, times) for d in range(1, times)]
    later = {"tm": tm + GROUP}
    barrier = pltpu.get_barrier_semaphore()
    targets = [{"mesh": m} for m in plane] + [{"tm": t} for t in column]
    for target in targets:
        pl.semaphore_signal(barrier, inc=1, device_id=target, device_id_type=MESH_ID)

    blocks = Blocks(a_ref, c_ref, r_ref, x_ref, shift_ref, couple_ref)
    parts = (d_ref, e_ref, u_ref, h_ref, g_ref)
    local_blocks(blocks, *parts)
    pl.semaphore_wait(barrier, len(targets))

    def copies(s_src, w_src):
        return [
            pltpu.make_async_remote_copy(
                src_ref=src, dst_ref=dst, send_sem=send.at[i], recv_sem=recv.at[i],
                device_id=later, device_id_type=MESH_ID,
            )
            for i, (src, dst) in enumerate([(s_src, sin_ref), (w_src, win_ref)])
        ]

    @pl.when(seg == 0)
    def _():
        out = copies(d_ref.at[2], h_ref.at[2])
        for copy in out:
            copy.start()
        sin_ref[...] = eye128()
        win_ref[...] = jnp.zeros((HROWS, 128), F32)

    @pl.when(seg > 0)
    def _():
        out = copies(s_out, w_out)
        out[0].wait_recv()

        @pl.when(seg < segs - 1)
        def _():
            (inverse,), _ = inverse_factors([sin_ref[...] - u_ref[2]], 16)
            half = dot_nt(e_ref[2], inverse)
            s_out[...] = d_ref[2] - dot_nt(half, half)
            out[0].start()
            out[1].wait_recv()
            w_out[...] = h_ref[2] - dot_nt(dot_nt(win_ref[...] + g_ref[2], inverse), half)
            out[1].start()

    def wait_w():
        @pl.when(seg == segs - 1)
        def _():
            copies(s_out, w_out)[1].wait_recv()

    finish_blocks(chunks, blocks, sin_ref, win_ref, wait_w, *parts, gram_ref, lf_ref)

    one = [
        start_copy(gram_ref.at[m], one_in.at[me], one_s.at[d], one_r.at[d], {"mesh": m})
        for d, m in enumerate(plane)
    ]
    one_in[me] = gram_ref[me]
    for copy in one:
        copy.wait_recv()
    total = one_in[0]
    for m in range(1, chunks):
        total = total + one_in[m]
    one_out[...] = total
    two_in[tm] = total
    two = [
        start_copy(one_out, two_in.at[tm], two_s.at[d], two_r.at[d], {"tm": t})
        for d, t in enumerate(column)
    ]
    lf = [
        start_copy(lf_ref.at[lax.rem(slot + d + 1, GROUP)], lf_in.at[slot], lf_s.at[d], lf_r.at[d], {"tm": t})
        for d, t in enumerate(group)
    ]
    lf_in[slot] = lf_ref[slot]
    for copy in two:
        copy.wait_recv()
    rows = 64 // chunks
    for c in range(GROUP):
        total = two_in[c]
        for t in range(c + GROUP, times, GROUP):
            total = total + two_in[t]
        two_out[rows * c : rows * (c + 1), :] = total[0:rows, :]
    three = [
        start_copy(two_out, three_in.at[me], three_s.at[d], three_r.at[d], {"mesh": m})
        for d, m in enumerate(plane)
    ]
    three_in[me] = two_out[...]
    for copy in lf + three:
        copy.wait_recv()

    @pl.when(seg < segs - 1)
    def _():
        for copy in copies(s_out, w_out):
            copy.wait_send()

    for copy in one + two + lf + three:
        copy.wait_send()


def main_phase(gathered, config_shift, config_coupling, chunks, times):
    dma = pltpu.SemaphoreType.DMA
    rows = GROUP * 64 // chunks
    tile, strip = (128, 128), (HROWS, 128)
    return pl.pallas_call(
        functools.partial(main_kernel, chunks, times),
        out_shape=(
            jax.ShapeDtypeStruct((GROUP, 8, 128), F32),
            jax.ShapeDtypeStruct((chunks, rows, 128), F32),
        ),
        in_specs=[vspec()] * 4 + [sspec()] * 2,
        out_specs=(vspec(),) * 2,
        scratch_shapes=[VM((3,) + tile, F32)] * 3
        + [VM((3,) + strip, F32)] * 2
        + [VM(tile, F32), VM(strip, F32)] * 2
        + [
            VM((chunks, 8, 128), F32),
            VM((GROUP, 8, 128), F32),
            VM((chunks, 8, 128), F32),
            VM((times, 8, 128), F32),
            VM((8, 128), F32),
            VM((rows, 128), F32),
        ]
        + [dma((2,))] * 2
        + [dma((GROUP - 1,))] * 2
        + [dma((chunks - 1,))] * 2
        + [dma((times - 1,))] * 2
        + [dma((chunks - 1,))] * 2,
        compiler_params=pltpu.CompilerParams(collective_id=1, has_side_effects=True),
    )(*gathered, config_shift, config_coupling)


def tip_kernel(chunks, lf_ref, sum_ref, diag_ref, rhs_ref, log_ref, fwd_ref, tlog_ref, tfwd_ref):
    sub = lax.broadcasted_iota(jnp.int32, (8, 128), 0)
    lane = lax.broadcasted_iota(jnp.int32, (8, 128), 1)
    pad = jnp.zeros((1, 64), F32)
    diag = jnp.concatenate([diag_ref[...], pad], axis=1)
    rhs = jnp.concatenate([rhs_ref[...], pad], axis=1)
    rows = 64 // chunks
    start = []
    for i in range(8):
        on = lane == sub + 8 * i
        column = jnp.sum(jnp.where(on, rhs, 0.0), axis=1, keepdims=True)
        start.append(jnp.where(on, diag, 0.0) + jnp.where(lane == 64, column, 0.0))
    mats = []
    for c in range(GROUP):
        log_ref[c] = lf_ref[c, 0:1, :]
        fwd_ref[c] = lf_ref[c, 1:2, :]
        whole = jnp.concatenate(
            [sum_ref[m, rows * c : rows * (c + 1), :] for m in range(chunks)], axis=0
        )
        mats.append([start[i] - whole[8 * i : 8 * i + 8, :] for i in range(8)])
    done, pivots = factor(mats, 64, 8)
    for c in range(GROUP):
        logs = jnp.zeros((8, 128), F32)
        solved = jnp.zeros((8, 128), F32)
        for i in range(8):
            on = lane == sub + 8 * i
            logs = logs + jnp.where(on, jnp.log(pivots[c][i]), 0.0)
            solved = solved + jnp.where(on, lane_of(done[c][i], 64) * lax.rsqrt(pivots[c][i]), 0.0)
        tlog_ref[c : c + 1, :] = 0.5 * jnp.sum(logs, axis=0, keepdims=True)[:, 0:64]
        tfwd_ref[c : c + 1, :] = jnp.sum(solved, axis=0, keepdims=True)[:, 0:64]


def tip_phase(lf, summed, tip_diag, tip_rhs, chunks):
    wide = jax.ShapeDtypeStruct((GROUP, 1, 128), F32)
    narrow = jax.ShapeDtypeStruct((GROUP, 64), F32)
    return pl.pallas_call(
        functools.partial(tip_kernel, chunks),
        out_shape=(wide, wide, narrow, narrow),
        in_specs=[vspec()] * 4,
        out_specs=(vspec(),) * 4,
    )(lf, summed, tip_diag[None], tip_rhs[None])


def shards(
    diag_blocks, coupling, arrow_cols, rhs, tip_rhs, tip_diag, config_shift, config_coupling, pattern
):
    times, chunks = lax.axis_size("tm"), lax.axis_size("mesh")
    gathered = group_gather(pattern, diag_blocks, coupling, arrow_cols, rhs)
    lf, summed = main_phase(gathered, config_shift, config_coupling, chunks, times)
    return tip_phase(lf, summed, tip_diag, tip_rhs, chunks)


def solution(mesh):
    in_specs = (
        P("tm", "mesh", None),
        P("tm", "mesh", None),
        P("tm", None, "mesh"),
        P("tm", "mesh"),
        P(),
        P(),
        P(),
        P(),
        P("tm", "mesh"),
    )
    out_specs = (P(None, "tm", "mesh"), P(None, "tm", "mesh"), P(), P())
    return jax.shard_map(shards, mesh=mesh, in_specs=in_specs, out_specs=out_specs, check_vma=False)
```

```python
import functools

import jax
import jax.numpy as jnp
from jax import lax
from jax.experimental import pallas as pl
from jax.experimental.pallas import tpu as pltpu
from jax.sharding import PartitionSpec as P

F32 = jnp.float32
GROUP = 4
HROWS = 72
MESH_ID = pl.DeviceIdType.MESH
VM = pltpu.VMEM
NT = (((1,), (1,)), ((), ()))
NN = (((1,), (0,)), ((), ()))


def vspec():
    return pl.BlockSpec(memory_space=pltpu.VMEM)


def sspec():
    return pl.BlockSpec(memory_space=pltpu.SMEM)


def halves(x):
    high = x.astype(jnp.bfloat16)
    return high, (x - high.astype(F32)).astype(jnp.bfloat16)


def product(a, b, dims):
    ah, al = halves(a)
    bh, bl = halves(b)

    def one(x, y):
        return lax.dot_general(x, y, dims, preferred_element_type=F32)

    return one(ah, bh) + (one(ah, bl) + one(al, bh))


def dot_nt(a, b):
    return product(a, b, NT)


def lane_of(x, j):
    return jnp.broadcast_to(x[:, j : j + 1], x.shape)


def row_of(x, k):
    return jnp.broadcast_to(x[k : k + 1, :], x.shape)


def factor(mats, rows, width):
    tiles, wide = rows // 8, width // 8
    sub = lax.broadcasted_iota(jnp.int32, (8, 128), 0)
    lane = lax.broadcasted_iota(jnp.int32, (8, 128), 1)
    is_row = [sub == k for k in range(8)]
    mats = [list(m) for m in mats]
    pivots = [[None] * tiles for _ in mats]
    for base in range(0, rows, width):
        first = base // 8
        inside = (lane >= base) & (lane < base + width)
        state = []
        for mat in mats:
            panel = [mat[first + u] for u in range(wide)]
            cols = [[lane_of(panel[u], base + j) for u in range(wide)] for j in range(width)]
            panel = [
                jnp.where(inside, jnp.where(lane - base - 8 * u == sub, 1.0, 0.0), panel[u])
                for u in range(wide)
            ]
            ahead = None
            if first + wide < tiles:
                ahead = [
                    [lane_of(mat[first + wide + u], base + j) for j in range(width)]
                    for u in range(wide)
                ]
            state.append((panel, cols, list(panel), [jnp.ones((8, 128), F32)] * wide, ahead))
        for k in range(width):
            tile, row = divmod(k, 8)
            mine = is_row[row]
            for panel, cols, done, piv, _ in state:
                pivot = row_of(cols[k][tile], row)
                inv = 1.0 / pivot
                kept = row_of(panel[tile], row)
                done[tile] = jnp.where(mine, kept, done[tile])
                piv[tile] = jnp.where(mine, pivot, piv[tile])
                kept = kept * inv
                own = cols[k]
                for u in range(wide):
                    new = panel[u] - own[u] * kept
                    panel[u] = jnp.where(mine, kept, new) if u == tile else new
                for j in range(k + 1, width):
                    mult = row_of(cols[j][tile], row) * inv
                    for u in range(wide):
                        new = cols[j][u] - own[u] * mult
                        cols[j][u] = jnp.where(mine, mult, new) if u == tile else new
        for (panel, cols, done, piv, ahead), mat, pivs in zip(state, mats, pivots):
            start = first + wide
            if start < tiles:
                spread = [row_of(panel[j // 8], j % 8) for j in range(width)]
                for u in range(wide):
                    terms = [ahead[u][j] * spread[j] for j in range(width)]
                    while len(terms) > 1:
                        terms = [x + y for x, y in zip(terms[::2], terms[1::2])]
                    mat[start + u] = jnp.where(inside, 0.0, mat[start + u]) - terms[0]
                start += wide
            if start < tiles:
                zero = jnp.zeros((8, 128), F32)
                left = jnp.concatenate([jnp.where(inside, mat[q], 0.0) for q in range(start, tiles)], axis=0)
                right = jnp.concatenate([zero] * first + panel + [zero] * (16 - first - wide), axis=0)
                update = product(left, right, NN)
                for q in range(start, tiles):
                    row = 8 * (q - start)
                    mat[q] = jnp.where(inside, 0.0, mat[q]) - update[row : row + 8, :]
            for u in range(wide):
                mat[first + u] = done[u]
                pivs[first + u] = piv[u]
    return mats, pivots


def inverse_factors(mats, width):
    sub = lax.broadcasted_iota(jnp.int32, (8, 128), 0)
    lane = lax.broadcasted_iota(jnp.int32, (8, 128), 1)
    tiled = [[m[8 * i : 8 * i + 8, :] for i in range(16)] for m in mats]
    done, pivots = factor(tiled, 128, width)
    inverses = [
        jnp.concatenate(
            [
                jnp.where(lane <= sub + 8 * i, d[i] * lax.rsqrt(p[i]), 0.0)
                for i in range(16)
            ],
            axis=0,
        )
        for d, p in zip(done, pivots)
    ]
    return inverses, pivots


def eye128():
    sub = lax.broadcasted_iota(jnp.int32, (128, 128), 0)
    lane = lax.broadcasted_iota(jnp.int32, (128, 128), 1)
    return jnp.where(sub == lane, 1.0, 0.0)


def eliminate(mats, stacks, width):
    inverses, _ = inverse_factors(mats, width)
    out = []
    for stack, inv in zip(stacks, inverses):
        half = dot_nt(stack, inv)
        out.append(dot_nt(half, half[: half.shape[0] - HROWS]))
    return out


def gather_kernel(
    pat_ref, a_ref, c_ref, r_ref, y_ref, ao_ref, co_ref, ro_ref, xo_ref, x_ref,
    near_s, near_r, far_s, far_r, pass_s, pass_r, own,
):
    me = lax.axis_index("tm")
    slot = lax.rem(me, GROUP)
    base = me - slot
    core = lax.rem(slot, 2)
    far_slot = lax.rem(slot + 2, GROUP)
    near = {"tm": me + 1 - 2 * core}
    far = {"tm": base + far_slot}
    barrier = pltpu.get_barrier_semaphore()
    for peer in (near, far):
        pl.semaphore_signal(barrier, inc=1, device_id=peer, device_id_type=MESH_ID)
    x_ref[...] = jnp.zeros((8, 128), F32)
    x_ref[0:1, :] = y_ref[...]
    keep = jnp.where(me > 0, pat_ref[0, 0], 0).astype(F32)
    x_ref[1:2, :] = jnp.full((1, 128), 1.0, F32) * keep
    pl.semaphore_wait(barrier, 2)
    outs = (ao_ref, co_ref, ro_ref, xo_ref)
    mine = (a_ref.at[0], c_ref.at[0], r_ref.at[0], x_ref)

    def send(src, dst, ss, rs, target):
        copy = pltpu.make_async_remote_copy(
            src_ref=src, dst_ref=dst, send_sem=ss, recv_sem=rs, device_id=target, device_id_type=MESH_ID
        )
        copy.start()
        return copy

    far_copies = [
        send(mine[i], outs[i].at[slot], far_s.at[i], far_r.at[i], far) for i in range(4)
    ]
    near_copies = [
        send(mine[i], outs[i].at[slot], near_s.at[i], near_r.at[i], near) for i in range(4)
    ]
    local = [pltpu.make_async_copy(mine[i], outs[i].at[slot], own.at[i]) for i in range(4)]
    for copy in local:
        copy.start()
    passed = []
    for i in range(4):
        far_copies[i].wait_recv()
        passed.append(
            send(outs[i].at[far_slot], outs[i].at[far_slot], pass_s.at[i], pass_r.at[i], near)
        )
    for copy in local:
        copy.wait()
    for copy in far_copies:
        copy.wait_send()
    for copy in near_copies + passed:
        copy.wait()


def group_gather(pattern, diag_blocks, coupling, arrow_cols, rhs):
    dma = pltpu.SemaphoreType.DMA
    return pl.pallas_call(
        gather_kernel,
        out_shape=(
            jax.ShapeDtypeStruct((GROUP, 128, 128), F32),
            jax.ShapeDtypeStruct((GROUP, 128, 128), F32),
            jax.ShapeDtypeStruct((GROUP, 64, 128), F32),
            jax.ShapeDtypeStruct((GROUP, 8, 128), F32),
        ),
        in_specs=[sspec()] + [vspec()] * 4,
        out_specs=(vspec(),) * 4,
        scratch_shapes=[VM((8, 128), F32)] + [dma((4,))] * 7,
        compiler_params=pltpu.CompilerParams(collective_id=0, has_side_effects=True),
    )(pattern, diag_blocks, coupling, arrow_cols, rhs)


class Blocks:
    def __init__(self, a_ref, c_ref, r_ref, x_ref, shift_ref, couple_ref):
        slot = lax.rem(lax.axis_index("tm"), GROUP)
        self.refs = (a_ref, c_ref, r_ref, x_ref)
        self.shift, self.couple = shift_ref[slot], couple_ref[slot]

    def diag(self, i):
        return self.refs[0][i] + self.shift * eye128()

    def coup(self, i):
        return self.refs[1][i] * (self.refs[3][i, 1:2, :] * self.couple)

    def right(self, i):
        x = self.refs[3][i]
        sub = lax.broadcasted_iota(jnp.int32, (8, 128), 0)
        return jnp.concatenate([self.refs[2][i], jnp.where(sub == 0, x, 0.0)], axis=0)


def local_blocks(blocks, send_state, send_right, d_ref, e_ref, u_ref, h_ref, g_ref):
    diag, coup, right = blocks.diag, blocks.coup, blocks.right
    m0 = jnp.concatenate([coup(1), coup(0), right(0)], axis=0)
    m2 = jnp.concatenate([coup(3), coup(2), right(2)], axis=0)
    ga, gb = eliminate([diag(0), diag(2)], [m0, m2], 8)
    d1 = diag(1) - ga[0:128, 0:128]
    ub = gb[128:256, 128:256]
    (inv_c, inv_d), _ = inverse_factors([d1, d1 - ub], 8)
    eb = -gb[0:128, 128:256]
    half_e = dot_nt(eb, inv_d)
    d_ref[2] = diag(3) - gb[0:128, 0:128] - dot_nt(half_e, half_e)
    send_state()
    h1 = right(1) - ga[256:328, 0:128]
    gvb = -gb[256:328, 128:256]
    half_h = dot_nt(h1 + gvb, inv_d)
    h_ref[2] = right(3) - gb[256:328, 0:128] - dot_nt(half_h, half_e)
    send_right()
    u1 = ga[128:256, 128:256]
    et1 = -ga[128:256, 0:128]
    g1 = -ga[256:328, 128:256]
    half_t = dot_nt(et1, inv_d)
    e_ref[2] = -dot_nt(half_e, half_t)
    u_ref[2] = u1 + dot_nt(half_t, half_t)
    g_ref[2] = g1 - dot_nt(half_h, half_t)
    d_ref[0] = d1
    e_ref[0] = -ga[0:128, 128:256]
    u_ref[0] = u1
    h_ref[0] = h1
    g_ref[0] = g1
    half = dot_nt(jnp.concatenate([coup(2), et1, h1], axis=0), inv_c)
    gc = dot_nt(half, half[0:256])
    d_ref[1] = diag(2) - gc[0:128, 0:128]
    e_ref[1] = -gc[0:128, 128:256]
    u_ref[1] = u1 + gc[128:256, 128:256]
    h_ref[1] = right(2) - gc[256:328, 0:128]
    g_ref[1] = g1 - gc[256:328, 128:256]


def start_copy(src, dst, ss, rs, target):
    copy = pltpu.make_async_remote_copy(
        src_ref=src, dst_ref=dst, send_sem=ss, recv_sem=rs, device_id=target, device_id_type=MESH_ID
    )
    copy.start()
    return copy


def finish_blocks(chunks, blocks, sin_ref, win_ref, wait_w, d_ref, e_ref, u_ref, h_ref, g_ref, gram_ref, lf_ref):
    sub = lax.broadcasted_iota(jnp.int32, (8, 128), 0)
    lane = lax.broadcasted_iota(jnp.int32, (8, 128), 1)
    before = sin_ref[...]
    inverses, _ = inverse_factors([before] + [before - u_ref[i] for i in range(3)], 8)
    wait_w()
    w = win_ref[...]
    stacks = [jnp.concatenate([blocks.coup(0), w], axis=0)] + [
        jnp.concatenate([e_ref[i], w + g_ref[i]], axis=0) for i in range(3)
    ]
    diags = [blocks.diag(0)] + [d_ref[i] for i in range(3)]
    rights = [blocks.right(0)] + [h_ref[i] for i in range(3)]
    schur, whole = [], []
    for stack, inv, d, h in zip(stacks, inverses, diags, rights):
        half = dot_nt(stack, inv)
        gram = dot_nt(half, half[0:128])
        schur.append(d - gram[0:128])
        whole.append(h - gram[128:200])
    inverses, pivots = inverse_factors(schur, 8)
    total = None
    for i in range(GROUP):
        x = dot_nt(whole[i], inverses[i])
        gram = dot_nt(x, x)
        total = gram if total is None else total + gram
        logs = jnp.zeros((8, 128), F32)
        for k in range(16):
            logs = logs + jnp.where(lane == sub + 8 * k, jnp.log(pivots[i][k]), 0.0)
        lf_ref[i] = jnp.where(
            sub == 0,
            0.5 * jnp.sum(logs, axis=0, keepdims=True),
            jnp.where(sub == 1, x[64:65, :], 0.0),
        )
    rows = 64 // chunks
    total = jnp.concatenate([total, jnp.zeros((HROWS, 128 - HROWS), F32)], axis=1)
    for m in range(chunks):
        gram_ref[m] = jnp.concatenate(
            [total[rows * m : rows * (m + 1), :], jnp.zeros((8 - rows, 128), F32)], axis=0
        )


def main_kernel(
    chunks, times, a_ref, c_ref, r_ref, x_ref, shift_ref, couple_ref, lf_in, three_in,
    d_ref, e_ref, u_ref, h_ref, g_ref, sin_ref, win_ref, s_out, w_out, gram_ref, lf_ref,
    one_in, two_in, acc_in, one_out, two_out, send, recv, acc_s, acc_r,
    lf_s, lf_r, one_s, one_r, two_s, two_r, three_s, three_r,
):
    tm, me = lax.axis_index("tm"), lax.axis_index("mesh")
    slot = lax.rem(tm, GROUP)
    seg = tm // GROUP
    segs = times // GROUP
    group = [tm - slot + lax.rem(slot + d, GROUP) for d in range(1, GROUP)]
    plane = [lax.rem(me + d, chunks) for d in range(1, chunks)]
    column = [lax.rem(tm + d, times) for d in range(1, times)]
    later = {"tm": tm + GROUP}
    earlier = {"tm": tm - GROUP}
    barrier = pltpu.get_barrier_semaphore()
    targets = [{"mesh": m} for m in plane] + [{"tm": t} for t in group]
    for target in targets:
        pl.semaphore_signal(barrier, inc=1, device_id=target, device_id_type=MESH_ID)

    @pl.when(seg > 0)
    def _():
        pl.semaphore_signal(barrier, inc=1, device_id=earlier, device_id_type=MESH_ID)

    @pl.when(seg < segs - 1)
    def _():
        pl.semaphore_signal(barrier, inc=1, device_id=later, device_id_type=MESH_ID)

    greeted = len(targets) + (seg > 0).astype(jnp.int32) + (seg < segs - 1).astype(jnp.int32)

    blocks = Blocks(a_ref, c_ref, r_ref, x_ref, shift_ref, couple_ref)
    parts = (d_ref, e_ref, u_ref, h_ref, g_ref)

    def copies(s_src, w_src):
        return [
            pltpu.make_async_remote_copy(
                src_ref=src, dst_ref=dst, send_sem=send.at[i], recv_sem=recv.at[i],
                device_id=later, device_id_type=MESH_ID,
            )
            for i, (src, dst) in enumerate([(s_src, sin_ref), (w_src, win_ref)])
        ]

    def send_state():
        pl.semaphore_wait(barrier, greeted)

        @pl.when(seg == 0)
        def _():
            copies(d_ref.at[2], h_ref.at[2])[0].start()
            sin_ref[...] = eye128()
            win_ref[...] = jnp.zeros((HROWS, 128), F32)
            acc_in[...] = jnp.zeros((8, 128), F32)

    def send_right():
        @pl.when(seg == 0)
        def _():
            copies(d_ref.at[2], h_ref.at[2])[1].start()

    local_blocks(blocks, send_state, send_right, *parts)

    @pl.when(seg > 0)
    def _():
        out = copies(s_out, w_out)
        out[0].wait_recv()

        @pl.when(seg < segs - 1)
        def _():
            (inverse,), _ = inverse_factors([sin_ref[...] - u_ref[2]], 16)
            half = dot_nt(e_ref[2], inverse)
            s_out[...] = d_ref[2] - dot_nt(half, half)
            out[0].start()
            out[1].wait_recv()
            w_out[...] = h_ref[2] - dot_nt(dot_nt(win_ref[...] + g_ref[2], inverse), half)
            out[1].start()

    def wait_w():
        @pl.when(seg == segs - 1)
        def _():
            copies(s_out, w_out)[1].wait_recv()

    finish_blocks(chunks, blocks, sin_ref, win_ref, wait_w, *parts, gram_ref, lf_ref)

    one = [
        start_copy(gram_ref.at[m], one_in.at[me], one_s.at[d], one_r.at[d], {"mesh": m})
        for d, m in enumerate(plane)
    ]
    one_in[me] = gram_ref[me]
    for copy in one:
        copy.wait_recv()
    total = one_in[0]
    for m in range(1, chunks):
        total = total + one_in[m]
    lf = [
        start_copy(lf_ref.at[lax.rem(slot + d + 1, GROUP)], lf_in.at[slot], lf_s.at[d], lf_r.at[d], {"tm": t})
        for d, t in enumerate(group)
    ]
    lf_in[slot] = lf_ref[slot]

    def pass_sum():
        return pltpu.make_async_remote_copy(
            src_ref=one_out, dst_ref=acc_in, send_sem=acc_s, recv_sem=acc_r,
            device_id=later, device_id_type=MESH_ID,
        )

    @pl.when(seg > 0)
    def _():
        pass_sum().wait_recv()

    total = total + acc_in[...]
    one_out[...] = total

    @pl.when(seg < segs - 1)
    def _():
        pass_sum().start()

    def spread():
        return [
            pltpu.make_async_remote_copy(
                src_ref=one_out, dst_ref=two_in.at[slot], send_sem=two_s.at[d], recv_sem=two_r.at[slot],
                device_id={"tm": t}, device_id_type=MESH_ID,
            )
            for d, t in enumerate(column)
        ]

    @pl.when(seg == segs - 1)
    def _():
        for copy in spread():
            copy.start()
        two_in[slot] = total

    for c in range(GROUP):
        @pl.when(tm != times - GROUP + c)
        def _():
            pltpu.make_async_remote_copy(
                src_ref=one_out, dst_ref=two_in.at[c], send_sem=two_s.at[0], recv_sem=two_r.at[c],
                device_id=later, device_id_type=MESH_ID,
            ).wait_recv()

    rows = 64 // chunks
    for c in range(GROUP):
        two_out[rows * c : rows * (c + 1), :] = two_in[c, 0:rows, :]
    three = [
        start_copy(two_out, three_in.at[me], three_s.at[d], three_r.at[d], {"mesh": m})
        for d, m in enumerate(plane)
    ]
    three_in[me] = two_out[...]
    for copy in lf + three:
        copy.wait_recv()

    @pl.when(seg < segs - 1)
    def _():
        for copy in copies(s_out, w_out):
            copy.wait_send()
        pass_sum().wait_send()

    @pl.when(seg == segs - 1)
    def _():
        for copy in spread():
            copy.wait_send()

    for copy in one + lf + three:
        copy.wait_send()


def main_phase(gathered, config_shift, config_coupling, chunks, times):
    dma = pltpu.SemaphoreType.DMA
    rows = GROUP * 64 // chunks
    tile, strip = (128, 128), (HROWS, 128)
    return pl.pallas_call(
        functools.partial(main_kernel, chunks, times),
        out_shape=(
            jax.ShapeDtypeStruct((GROUP, 8, 128), F32),
            jax.ShapeDtypeStruct((chunks, rows, 128), F32),
        ),
        in_specs=[vspec()] * 4 + [sspec()] * 2,
        out_specs=(vspec(),) * 2,
        scratch_shapes=[VM((3,) + tile, F32)] * 3
        + [VM((3,) + strip, F32)] * 2
        + [VM(tile, F32), VM(strip, F32)] * 2
        + [
            VM((chunks, 8, 128), F32),
            VM((GROUP, 8, 128), F32),
            VM((chunks, 8, 128), F32),
            VM((GROUP, 8, 128), F32),
            VM((8, 128), F32),
            VM((8, 128), F32),
            VM((rows, 128), F32),
        ]
        + [dma((2,))] * 2
        + [dma] * 2
        + [dma((GROUP - 1,))] * 2
        + [dma((chunks - 1,))] * 2
        + [dma((times - 1,)), dma((GROUP,))]
        + [dma((chunks - 1,))] * 2,
        compiler_params=pltpu.CompilerParams(collective_id=1, has_side_effects=True),
    )(*gathered, config_shift, config_coupling)


def tip_kernel(chunks, lf_ref, sum_ref, diag_ref, rhs_ref, log_ref, fwd_ref, tlog_ref, tfwd_ref):
    sub = lax.broadcasted_iota(jnp.int32, (8, 128), 0)
    lane = lax.broadcasted_iota(jnp.int32, (8, 128), 1)
    pad = jnp.zeros((1, 64), F32)
    diag = jnp.concatenate([diag_ref[...], pad], axis=1)
    rhs = jnp.concatenate([rhs_ref[...], pad], axis=1)
    rows = 64 // chunks
    start = []
    for i in range(8):
        on = lane == sub + 8 * i
        column = jnp.sum(jnp.where(on, rhs, 0.0), axis=1, keepdims=True)
        start.append(jnp.where(on, diag, 0.0) + jnp.where(lane == 64, column, 0.0))
    mats = []
    for c in range(GROUP):
        log_ref[c] = lf_ref[c, 0:1, :]
        fwd_ref[c] = lf_ref[c, 1:2, :]
        whole = jnp.concatenate(
            [sum_ref[m, rows * c : rows * (c + 1), :] for m in range(chunks)], axis=0
        )
        mats.append([start[i] - whole[8 * i : 8 * i + 8, :] for i in range(8)])
    done, pivots = factor(mats, 64, 8)
    for c in range(GROUP):
        logs = jnp.zeros((8, 128), F32)
        solved = jnp.zeros((8, 128), F32)
        for i in range(8):
            on = lane == sub + 8 * i
            logs = logs + jnp.where(on, jnp.log(pivots[c][i]), 0.0)
            solved = solved + jnp.where(on, lane_of(done[c][i], 64) * lax.rsqrt(pivots[c][i]), 0.0)
        tlog_ref[c : c + 1, :] = 0.5 * jnp.sum(logs, axis=0, keepdims=True)[:, 0:64]
        tfwd_ref[c : c + 1, :] = jnp.sum(solved, axis=0, keepdims=True)[:, 0:64]


def tip_phase(lf, summed, tip_diag, tip_rhs, chunks):
    wide = jax.ShapeDtypeStruct((GROUP, 1, 128), F32)
    narrow = jax.ShapeDtypeStruct((GROUP, 64), F32)
    return pl.pallas_call(
        functools.partial(tip_kernel, chunks),
        out_shape=(wide, wide, narrow, narrow),
        in_specs=[vspec()] * 4,
        out_specs=(vspec(),) * 4,
    )(lf, summed, tip_diag[None], tip_rhs[None])


def shards(
    diag_blocks, coupling, arrow_cols, rhs, tip_rhs, tip_diag, config_shift, config_coupling, pattern
):
    times, chunks = lax.axis_size("tm"), lax.axis_size("mesh")
    gathered = group_gather(pattern, diag_blocks, coupling, arrow_cols, rhs)
    lf, summed = main_phase(gathered, config_shift, config_coupling, chunks, times)
    return tip_phase(lf, summed, tip_diag, tip_rhs, chunks)


def solution(mesh):
    in_specs = (
        P("tm", "mesh", None),
        P("tm", "mesh", None),
        P("tm", None, "mesh"),
        P("tm", "mesh"),
        P(),
        P(),
        P(),
        P(),
        P("tm", "mesh"),
    )
    out_specs = (P(None, "tm", "mesh"), P(None, "tm", "mesh"), P(), P())
    return jax.shard_map(shards, mesh=mesh, in_specs=in_specs, out_specs=out_specs, check_vma=False)
```

```python
import functools

import jax
import jax.numpy as jnp
from jax import lax
from jax.experimental import pallas as pl
from jax.experimental.pallas import tpu as pltpu
from jax.sharding import PartitionSpec as P

F32 = jnp.float32
GROUP = 4
HROWS = 72
MESH_ID = pl.DeviceIdType.MESH
VM = pltpu.VMEM
NT = (((1,), (1,)), ((), ()))
NN = (((1,), (0,)), ((), ()))


def vspec():
    return pl.BlockSpec(memory_space=pltpu.VMEM)


def sspec():
    return pl.BlockSpec(memory_space=pltpu.SMEM)


def halves(x):
    high = x.astype(jnp.bfloat16)
    return high, (x - high.astype(F32)).astype(jnp.bfloat16)


def product(a, b, dims):
    ah, al = halves(a)
    bh, bl = halves(b)

    def one(x, y):
        return lax.dot_general(x, y, dims, preferred_element_type=F32)

    return one(ah, bh) + (one(ah, bl) + one(al, bh))


def dot_nt(a, b):
    return product(a, b, NT)


def lane_of(x, j):
    return jnp.broadcast_to(x[:, j : j + 1], x.shape)


def row_of(x, k):
    return jnp.broadcast_to(x[k : k + 1, :], x.shape)


def factor(mats, rows, width):
    tiles, wide = rows // 8, width // 8
    sub = lax.broadcasted_iota(jnp.int32, (8, 128), 0)
    lane = lax.broadcasted_iota(jnp.int32, (8, 128), 1)
    is_row = [sub == k for k in range(8)]
    mats = [list(m) for m in mats]
    pivots = [[None] * tiles for _ in mats]
    for base in range(0, rows, width):
        first = base // 8
        inside = (lane >= base) & (lane < base + width)
        state = []
        for mat in mats:
            panel = [mat[first + u] for u in range(wide)]
            cols = [[lane_of(panel[u], base + j) for u in range(wide)] for j in range(width)]
            panel = [
                jnp.where(inside, jnp.where(lane - base - 8 * u == sub, 1.0, 0.0), panel[u])
                for u in range(wide)
            ]
            ahead = None
            if first + wide < tiles:
                ahead = [
                    [lane_of(mat[first + wide + u], base + j) for j in range(width)]
                    for u in range(wide)
                ]
            state.append((panel, cols, list(panel), [jnp.ones((8, 128), F32)] * wide, ahead))
        for k in range(width):
            tile, row = divmod(k, 8)
            mine = is_row[row]
            for panel, cols, done, piv, _ in state:
                inv = row_of(1.0 / cols[k][tile], row)
                done[tile] = jnp.where(mine, panel[tile], done[tile])
                piv[tile] = jnp.where(mine, cols[k][tile], piv[tile])
                kept = row_of(panel[tile], row) * inv
                own = list(cols[k])
                own[tile] = jnp.where(mine, own[tile] - 1.0, own[tile])
                for u in range(wide):
                    panel[u] = panel[u] - own[u] * kept
                for j in range(k + 1, width):
                    mult = row_of(cols[j][tile], row) * inv
                    for u in range(wide):
                        cols[j][u] = cols[j][u] - own[u] * mult
        for (panel, cols, done, piv, ahead), mat, pivs in zip(state, mats, pivots):
            start = first + wide
            if start < tiles:
                spread = [row_of(panel[j // 8], j % 8) for j in range(width)]
                for u in range(wide):
                    terms = [ahead[u][j] * spread[j] for j in range(width)]
                    while len(terms) > 1:
                        terms = [x + y for x, y in zip(terms[::2], terms[1::2])]
                    mat[start + u] = jnp.where(inside, 0.0, mat[start + u]) - terms[0]
                start += wide
            if start < tiles:
                zero = jnp.zeros((8, 128), F32)
                left = jnp.concatenate([jnp.where(inside, mat[q], 0.0) for q in range(start, tiles)], axis=0)
                right = jnp.concatenate([zero] * first + panel + [zero] * (16 - first - wide), axis=0)
                update = product(left, right, NN)
                for q in range(start, tiles):
                    row = 8 * (q - start)
                    mat[q] = jnp.where(inside, 0.0, mat[q]) - update[row : row + 8, :]
            for u in range(wide):
                mat[first + u] = done[u]
                pivs[first + u] = piv[u]
    return mats, pivots


def inverse_factors(mats, width):
    sub = lax.broadcasted_iota(jnp.int32, (8, 128), 0)
    lane = lax.broadcasted_iota(jnp.int32, (8, 128), 1)
    tiled = [[m[8 * i : 8 * i + 8, :] for i in range(16)] for m in mats]
    done, pivots = factor(tiled, 128, width)
    inverses = [
        jnp.concatenate(
            [
                jnp.where(lane <= sub + 8 * i, d[i] * lax.rsqrt(p[i]), 0.0)
                for i in range(16)
            ],
            axis=0,
        )
        for d, p in zip(done, pivots)
    ]
    return inverses, pivots


def eye128():
    sub = lax.broadcasted_iota(jnp.int32, (128, 128), 0)
    lane = lax.broadcasted_iota(jnp.int32, (128, 128), 1)
    return jnp.where(sub == lane, 1.0, 0.0)


def eliminate(mats, stacks, width):
    inverses, _ = inverse_factors(mats, width)
    out = []
    for stack, inv in zip(stacks, inverses):
        half = dot_nt(stack, inv)
        out.append(dot_nt(half, half[: half.shape[0] - HROWS]))
    return out


def gather_kernel(
    pat_ref, a_ref, c_ref, r_ref, y_ref, ao_ref, co_ref, ro_ref, xo_ref, x_ref,
    near_s, near_r, far_s, far_r, pass_s, pass_r, own,
):
    me = lax.axis_index("tm")
    slot = lax.rem(me, GROUP)
    base = me - slot
    core = lax.rem(slot, 2)
    far_slot = lax.rem(slot + 2, GROUP)
    near = {"tm": me + 1 - 2 * core}
    far = {"tm": base + far_slot}
    barrier = pltpu.get_barrier_semaphore()
    for peer in (near, far):
        pl.semaphore_signal(barrier, inc=1, device_id=peer, device_id_type=MESH_ID)
    x_ref[...] = jnp.zeros((8, 128), F32)
    x_ref[0:1, :] = y_ref[...]
    keep = jnp.where(me > 0, pat_ref[0, 0], 0).astype(F32)
    x_ref[1:2, :] = jnp.full((1, 128), 1.0, F32) * keep
    pl.semaphore_wait(barrier, 2)
    outs = (ao_ref, co_ref, ro_ref, xo_ref)
    mine = (a_ref.at[0], c_ref.at[0], r_ref.at[0], x_ref)

    def send(src, dst, ss, rs, target):
        copy = pltpu.make_async_remote_copy(
            src_ref=src, dst_ref=dst, send_sem=ss, recv_sem=rs, device_id=target, device_id_type=MESH_ID
        )
        copy.start()
        return copy

    far_copies = [
        send(mine[i], outs[i].at[slot], far_s.at[i], far_r.at[i], far) for i in range(4)
    ]
    near_copies = [
        send(mine[i], outs[i].at[slot], near_s.at[i], near_r.at[i], near) for i in range(4)
    ]
    local = [pltpu.make_async_copy(mine[i], outs[i].at[slot], own.at[i]) for i in range(4)]
    for copy in local:
        copy.start()
    passed = []
    for i in range(4):
        far_copies[i].wait_recv()
        passed.append(
            send(outs[i].at[far_slot], outs[i].at[far_slot], pass_s.at[i], pass_r.at[i], near)
        )
    for copy in local:
        copy.wait()
    for copy in far_copies:
        copy.wait_send()
    for copy in near_copies + passed:
        copy.wait()


def group_gather(pattern, diag_blocks, coupling, arrow_cols, rhs):
    dma = pltpu.SemaphoreType.DMA
    return pl.pallas_call(
        gather_kernel,
        out_shape=(
            VM((GROUP, 128, 128), F32),
            VM((GROUP, 128, 128), F32),
            VM((GROUP, 64, 128), F32),
            VM((GROUP, 8, 128), F32),
        ),
        in_specs=[sspec()] + [vspec()] * 4,
        out_specs=(vspec(),) * 4,
        scratch_shapes=[VM((8, 128), F32)] + [dma((4,))] * 7,
        compiler_params=pltpu.CompilerParams(collective_id=0, has_side_effects=True),
    )(pattern, diag_blocks, coupling, arrow_cols, rhs)


class Blocks:
    def __init__(self, a_ref, c_ref, r_ref, x_ref, shift_ref, couple_ref):
        slot = lax.rem(lax.axis_index("tm"), GROUP)
        self.refs = (a_ref, c_ref, r_ref, x_ref)
        self.shift, self.couple = shift_ref[slot], couple_ref[slot]

    def diag(self, i):
        return self.refs[0][i] + self.shift * eye128()

    def coup(self, i):
        return self.refs[1][i] * (self.refs[3][i, 1:2, :] * self.couple)

    def right(self, i):
        x = self.refs[3][i]
        sub = lax.broadcasted_iota(jnp.int32, (8, 128), 0)
        return jnp.concatenate([self.refs[2][i], jnp.where(sub == 0, x, 0.0)], axis=0)


def local_blocks(blocks, send_state, send_right, d_ref, e_ref, u_ref, h_ref, g_ref):
    diag, coup, right = blocks.diag, blocks.coup, blocks.right
    m0 = jnp.concatenate([coup(1), coup(0), right(0)], axis=0)
    m2 = jnp.concatenate([coup(3), coup(2), right(2)], axis=0)
    ga, gb = eliminate([diag(0), diag(2)], [m0, m2], 8)
    d1 = diag(1) - ga[0:128, 0:128]
    ub = gb[128:256, 128:256]
    (inv_c, inv_d), _ = inverse_factors([d1, d1 - ub], 8)
    eb = -gb[0:128, 128:256]
    half_e = dot_nt(eb, inv_d)
    d_ref[2] = diag(3) - gb[0:128, 0:128] - dot_nt(half_e, half_e)
    send_state()
    h1 = right(1) - ga[256:328, 0:128]
    gvb = -gb[256:328, 128:256]
    half_h = dot_nt(h1 + gvb, inv_d)
    h_ref[2] = right(3) - gb[256:328, 0:128] - dot_nt(half_h, half_e)
    send_right()
    u1 = ga[128:256, 128:256]
    et1 = -ga[128:256, 0:128]
    g1 = -ga[256:328, 128:256]
    half_t = dot_nt(et1, inv_d)
    e_ref[2] = -dot_nt(half_e, half_t)
    u_ref[2] = u1 + dot_nt(half_t, half_t)
    g_ref[2] = g1 - dot_nt(half_h, half_t)
    d_ref[0] = d1
    e_ref[0] = -ga[0:128, 128:256]
    u_ref[0] = u1
    h_ref[0] = h1
    g_ref[0] = g1
    half = dot_nt(jnp.concatenate([coup(2), et1, h1], axis=0), inv_c)
    gc = dot_nt(half, half[0:256])
    d_ref[1] = diag(2) - gc[0:128, 0:128]
    e_ref[1] = -gc[0:128, 128:256]
    u_ref[1] = u1 + gc[128:256, 128:256]
    h_ref[1] = right(2) - gc[256:328, 0:128]
    g_ref[1] = g1 - gc[256:328, 128:256]


def start_copy(src, dst, ss, rs, target):
    copy = pltpu.make_async_remote_copy(
        src_ref=src, dst_ref=dst, send_sem=ss, recv_sem=rs, device_id=target, device_id_type=MESH_ID
    )
    copy.start()
    return copy


def finish_blocks(blocks, sin_ref, win_ref, wait_w, d_ref, e_ref, u_ref, h_ref, g_ref, sum_ref, lf_ref):
    sub = lax.broadcasted_iota(jnp.int32, (8, 128), 0)
    lane = lax.broadcasted_iota(jnp.int32, (8, 128), 1)
    before = sin_ref[...]
    inverses, _ = inverse_factors([before] + [before - u_ref[i] for i in range(3)], 8)
    wait_w()
    w = win_ref[...]
    stacks = [jnp.concatenate([blocks.coup(0), w], axis=0)] + [
        jnp.concatenate([e_ref[i], w + g_ref[i]], axis=0) for i in range(3)
    ]
    diags = [blocks.diag(0)] + [d_ref[i] for i in range(3)]
    rights = [blocks.right(0)] + [h_ref[i] for i in range(3)]
    schur, whole = [], []
    for stack, inv, d, h in zip(stacks, inverses, diags, rights):
        half = dot_nt(stack, inv)
        gram = dot_nt(half, half[0:128])
        schur.append(d - gram[0:128])
        whole.append(h - gram[128:200])
    inverses, pivots = inverse_factors(schur, 8)
    total = None
    for i in range(GROUP):
        x = dot_nt(whole[i], inverses[i])
        gram = dot_nt(x, x)
        total = gram if total is None else total + gram
        logs = jnp.zeros((8, 128), F32)
        for k in range(16):
            logs = logs + jnp.where(lane == sub + 8 * k, jnp.log(pivots[i][k]), 0.0)
        lf_ref[i] = jnp.where(
            sub == 0,
            0.5 * jnp.sum(logs, axis=0, keepdims=True),
            jnp.where(sub == 1, x[64:65, :], 0.0),
        )
    total = jnp.concatenate([total, jnp.zeros((HROWS, 128 - HROWS), F32)], axis=1)
    wide_lane = lax.broadcasted_iota(jnp.int32, (32, 128), 1)
    sum_ref[0:32, :] = jnp.where(wide_lane < 64, total[0:32], pltpu.roll(total[32:64], 64, 1))
    sum_ref[32:40, :] = total[64:72]


def solve_tip(packed, tip_diag, tip_rhs):
    sub = lax.broadcasted_iota(jnp.int32, (8, 128), 0)
    lane = lax.broadcasted_iota(jnp.int32, (8, 128), 1)
    pad = jnp.zeros((1, 64), F32)
    diag = jnp.concatenate([tip_diag, pad], axis=1)
    rhs = jnp.concatenate([tip_rhs, pad], axis=1) - packed[32:33]
    gram = jnp.concatenate([packed[0:32], pltpu.roll(packed[0:32], 64, 1)], axis=0)
    mat = []
    for i in range(8):
        on = lane == sub + 8 * i
        column = jnp.sum(jnp.where(on, rhs, 0.0), axis=1, keepdims=True)
        own = jnp.where(on, diag, 0.0) - gram[8 * i : 8 * i + 8]
        mat.append(jnp.where(lane < 64, own, jnp.where(lane == 64, column, 0.0)))
    (done,), (pivots,) = factor([mat], 64, 8)
    logs = jnp.zeros((8, 128), F32)
    solved = jnp.zeros((8, 128), F32)
    for i in range(8):
        on = lane == sub + 8 * i
        logs = logs + jnp.where(on, jnp.log(pivots[i]), 0.0)
        solved = solved + jnp.where(on, lane_of(done[i], 64) * lax.rsqrt(pivots[i]), 0.0)
    logs = 0.5 * jnp.sum(logs, axis=0, keepdims=True)
    return jnp.where(sub == 0, logs, jnp.sum(solved, axis=0, keepdims=True))


def main_kernel(
    chunks, times, a_ref, c_ref, r_ref, x_ref, shift_ref, couple_ref, tdiag_ref, trhs_ref, lf_in, tip_in,
    d_ref, e_ref, u_ref, h_ref, g_ref, sin_ref, win_ref, s_out, w_out, sum_ref, lf_ref,
    plane_in, acc_in, tip_out, send, recv, acc_s, acc_r,
    lf_s, lf_r, plane_s, plane_r, tip_s, tip_r,
):
    tm, me = lax.axis_index("tm"), lax.axis_index("mesh")
    slot = lax.rem(tm, GROUP)
    seg = tm // GROUP
    segs = times // GROUP
    group = [tm - slot + lax.rem(slot + d, GROUP) for d in range(1, GROUP)]
    plane = [lax.rem(me + d, chunks) for d in range(1, chunks)]
    column = [lax.rem(tm + d, times) for d in range(1, times)]
    later = {"tm": tm + GROUP}
    earlier = {"tm": tm - GROUP}
    barrier = pltpu.get_barrier_semaphore()
    targets = [{"mesh": m} for m in plane] + [{"tm": t} for t in group]
    for target in targets:
        pl.semaphore_signal(barrier, inc=1, device_id=target, device_id_type=MESH_ID)

    @pl.when(seg > 0)
    def _():
        pl.semaphore_signal(barrier, inc=1, device_id=earlier, device_id_type=MESH_ID)

    @pl.when(seg < segs - 1)
    def _():
        pl.semaphore_signal(barrier, inc=1, device_id=later, device_id_type=MESH_ID)

    greeted = len(targets) + (seg > 0).astype(jnp.int32) + (seg < segs - 1).astype(jnp.int32)

    blocks = Blocks(a_ref, c_ref, r_ref, x_ref, shift_ref, couple_ref)
    parts = (d_ref, e_ref, u_ref, h_ref, g_ref)

    def copies(s_src, w_src):
        return [
            pltpu.make_async_remote_copy(
                src_ref=src, dst_ref=dst, send_sem=send.at[i], recv_sem=recv.at[i],
                device_id=later, device_id_type=MESH_ID,
            )
            for i, (src, dst) in enumerate([(s_src, sin_ref), (w_src, win_ref)])
        ]

    def send_state():
        pl.semaphore_wait(barrier, greeted)

        @pl.when(seg == 0)
        def _():
            copies(d_ref.at[2], h_ref.at[2])[0].start()
            sin_ref[...] = eye128()
            win_ref[...] = jnp.zeros((HROWS, 128), F32)
            acc_in[...] = jnp.zeros((40, 128), F32)

    def send_right():
        @pl.when(seg == 0)
        def _():
            copies(d_ref.at[2], h_ref.at[2])[1].start()

    local_blocks(blocks, send_state, send_right, *parts)

    @pl.when(seg > 0)
    def _():
        out = copies(s_out, w_out)
        out[0].wait_recv()

        @pl.when(seg < segs - 1)
        def _():
            (inverse,), _ = inverse_factors([sin_ref[...] - u_ref[2]], 8)
            half = dot_nt(e_ref[2], inverse)
            s_out[...] = d_ref[2] - dot_nt(half, half)
            out[0].start()
            out[1].wait_recv()
            w_out[...] = h_ref[2] - dot_nt(dot_nt(win_ref[...] + g_ref[2], inverse), half)
            out[1].start()

    def wait_w():
        @pl.when(seg == segs - 1)
        def _():
            copies(s_out, w_out)[1].wait_recv()

    finish_blocks(blocks, sin_ref, win_ref, wait_w, *parts, sum_ref, lf_ref)

    lf = [
        start_copy(lf_ref.at[lax.rem(slot + d + 1, GROUP)], lf_in.at[slot], lf_s.at[d], lf_r.at[d], {"tm": t})
        for d, t in enumerate(group)
    ]
    lf_in[slot] = lf_ref[slot]

    def pass_sum():
        return pltpu.make_async_remote_copy(
            src_ref=sum_ref, dst_ref=acc_in, send_sem=acc_s, recv_sem=acc_r,
            device_id=later, device_id_type=MESH_ID,
        )

    @pl.when(seg > 0)
    def _():
        pass_sum().wait_recv()

    total = sum_ref[...] + acc_in[...]
    sum_ref[...] = total

    @pl.when(seg < segs - 1)
    def _():
        pass_sum().start()

    @pl.when(seg == segs - 1)
    def _():
        share = [
            start_copy(sum_ref, plane_in.at[me], plane_s.at[d], plane_r.at[d], {"mesh": m})
            for d, m in enumerate(plane)
        ]
        plane_in[me] = total
        for copy in share:
            copy.wait_recv()
        whole = plane_in[0]
        for m in range(1, chunks):
            whole = whole + plane_in[m]
        result = solve_tip(whole, tdiag_ref[...], trhs_ref[...])
        tip_out[...] = result
        spread = [
            start_copy(tip_out, tip_in.at[slot], tip_s.at[d], tip_r.at[slot], {"tm": t})
            for d, t in enumerate(column)
        ]
        tip_in[slot] = result
        for copy in share + spread:
            copy.wait_send()

    for copy in lf:
        copy.wait()
    for c in range(GROUP):

        @pl.when(tm != times - GROUP + c)
        def _():
            pltpu.make_async_remote_copy(
                src_ref=tip_out, dst_ref=tip_in.at[c], send_sem=tip_s.at[0], recv_sem=tip_r.at[c],
                device_id=later, device_id_type=MESH_ID,
            ).wait_recv()

    @pl.when(seg < segs - 1)
    def _():
        for copy in copies(s_out, w_out):
            copy.wait_send()
        pass_sum().wait_send()


def main_phase(gathered, config_shift, config_coupling, tip_diag, tip_rhs, chunks, times):
    dma = pltpu.SemaphoreType.DMA
    tile, strip = (128, 128), (HROWS, 128)
    return pl.pallas_call(
        functools.partial(main_kernel, chunks, times),
        out_shape=(VM((GROUP, 8, 128), F32), VM((GROUP, 8, 128), F32)),
        in_specs=[vspec()] * 4 + [sspec()] * 2 + [vspec()] * 2,
        out_specs=(vspec(),) * 2,
        scratch_shapes=[VM((3,) + tile, F32)] * 3
        + [VM((3,) + strip, F32)] * 2
        + [VM(tile, F32), VM(strip, F32)] * 2
        + [
            VM((40, 128), F32),
            VM((GROUP, 8, 128), F32),
            VM((chunks, 40, 128), F32),
            VM((40, 128), F32),
            VM((8, 128), F32),
        ]
        + [dma((2,))] * 2
        + [dma] * 2
        + [dma((GROUP - 1,))] * 2
        + [dma((chunks - 1,))] * 2
        + [dma((times - 1,)), dma((GROUP,))],
        compiler_params=pltpu.CompilerParams(collective_id=1, has_side_effects=True),
    )(*gathered, config_shift, config_coupling, tip_diag[None], tip_rhs[None])


def write_kernel(lf_ref, tip_ref, log_ref, fwd_ref, tlog_ref, tfwd_ref):
    for c in range(GROUP):
        log_ref[c] = lf_ref[c, 0:1, :]
        fwd_ref[c] = lf_ref[c, 1:2, :]
        tlog_ref[c : c + 1, :] = tip_ref[c, 0:1, 0:64]
        tfwd_ref[c : c + 1, :] = tip_ref[c, 1:2, 0:64]


def write_phase(lf, tip):
    wide = jax.ShapeDtypeStruct((GROUP, 1, 128), F32)
    narrow = jax.ShapeDtypeStruct((GROUP, 64), F32)
    return pl.pallas_call(
        write_kernel,
        out_shape=(wide, wide, narrow, narrow),
        in_specs=[vspec()] * 2,
        out_specs=(vspec(),) * 4,
    )(lf, tip)


def shards(
    diag_blocks, coupling, arrow_cols, rhs, tip_rhs, tip_diag, config_shift, config_coupling, pattern
):
    times, chunks = lax.axis_size("tm"), lax.axis_size("mesh")
    gathered = group_gather(pattern, diag_blocks, coupling, arrow_cols, rhs)
    gathered = [pltpu.with_memory_space_constraint(v, pltpu.VMEM) for v in gathered]
    results = main_phase(gathered, config_shift, config_coupling, tip_diag, tip_rhs, chunks, times)
    return write_phase(*[pltpu.with_memory_space_constraint(v, pltpu.VMEM) for v in results])


def solution(mesh):
    in_specs = (
        P("tm", "mesh", None),
        P("tm", "mesh", None),
        P("tm", None, "mesh"),
        P("tm", "mesh"),
        P(),
        P(),
        P(),
        P(),
        P("tm", "mesh"),
    )
    out_specs = (P(None, "tm", "mesh"), P(None, "tm", "mesh"), P(), P())
    return jax.shard_map(shards, mesh=mesh, in_specs=in_specs, out_specs=out_specs, check_vma=False)
```

```python
import functools

import jax
import jax.numpy as jnp
from jax import lax
from jax.experimental import pallas as pl
from jax.experimental.pallas import tpu as pltpu
from jax.sharding import PartitionSpec as P

F32 = jnp.float32
GROUP = 4
HROWS = 72
MESH_ID = pl.DeviceIdType.MESH
VM = pltpu.VMEM
NT = (((1,), (1,)), ((), ()))
NN = (((1,), (0,)), ((), ()))


def vspec():
    return pl.BlockSpec(memory_space=pltpu.VMEM)


def sspec():
    return pl.BlockSpec(memory_space=pltpu.SMEM)


def halves(x):
    high = x.astype(jnp.bfloat16)
    return high, (x - high.astype(F32)).astype(jnp.bfloat16)


def product(a, b, dims):
    ah, al = halves(a)
    bh, bl = halves(b)

    def one(x, y):
        return lax.dot_general(x, y, dims, preferred_element_type=F32)

    return one(ah, bh) + (one(ah, bl) + one(al, bh))


def dot_nt(a, b):
    return product(a, b, NT)


def lane_of(x, j):
    return jnp.broadcast_to(x[:, j : j + 1], x.shape)


def row_of(x, k):
    return jnp.broadcast_to(x[k : k + 1, :], x.shape)


def factor(mats, rows, width):
    tiles, wide = rows // 8, width // 8
    sub = lax.broadcasted_iota(jnp.int32, (8, 128), 0)
    lane = lax.broadcasted_iota(jnp.int32, (8, 128), 1)
    is_row = [sub == k for k in range(8)]
    mats = [list(m) for m in mats]
    pivots = [[None] * tiles for _ in mats]
    for base in range(0, rows, width):
        first = base // 8
        inside = (lane >= base) & (lane < base + width)
        state = []
        for mat in mats:
            panel = [mat[first + u] for u in range(wide)]
            cols = [[lane_of(panel[u], base + j) for u in range(wide)] for j in range(width)]
            panel = [
                jnp.where(inside, jnp.where(lane - base - 8 * u == sub, 1.0, 0.0), panel[u])
                for u in range(wide)
            ]
            ahead = None
            if first + wide < tiles:
                ahead = [
                    [lane_of(mat[first + wide + u], base + j) for j in range(width)]
                    for u in range(wide)
                ]
            state.append((panel, cols, list(panel), [jnp.ones((8, 128), F32)] * wide, ahead))
        for k in range(width):
            tile, row = divmod(k, 8)
            mine = is_row[row]
            for panel, cols, done, piv, _ in state:
                inv = row_of(1.0 / cols[k][tile], row)
                done[tile] = jnp.where(mine, panel[tile], done[tile])
                piv[tile] = jnp.where(mine, cols[k][tile], piv[tile])
                own = list(cols[k])
                own[tile] = jnp.where(mine, own[tile] - 1.0, own[tile])
                own = [part * inv for part in own]
                kept = row_of(panel[tile], row)
                for u in range(wide):
                    panel[u] = panel[u] - own[u] * kept
                for j in range(k + 1, width):
                    kept = row_of(cols[j][tile], row)
                    for u in range(wide):
                        cols[j][u] = cols[j][u] - own[u] * kept
        for (panel, cols, done, piv, ahead), mat, pivs in zip(state, mats, pivots):
            start = first + wide
            if start < tiles:
                spread = [row_of(panel[j // 8], j % 8) for j in range(width)]
                for u in range(wide):
                    terms = [ahead[u][j] * spread[j] for j in range(width)]
                    while len(terms) > 1:
                        terms = [x + y for x, y in zip(terms[::2], terms[1::2])]
                    mat[start + u] = jnp.where(inside, 0.0, mat[start + u]) - terms[0]
                start += wide
            if start < tiles:
                zero = jnp.zeros((8, 128), F32)
                left = jnp.concatenate([jnp.where(inside, mat[q], 0.0) for q in range(start, tiles)], axis=0)
                right = jnp.concatenate([zero] * first + panel + [zero] * (16 - first - wide), axis=0)
                update = product(left, right, NN)
                for q in range(start, tiles):
                    row = 8 * (q - start)
                    mat[q] = jnp.where(inside, 0.0, mat[q]) - update[row : row + 8, :]
            for u in range(wide):
                mat[first + u] = done[u]
                pivs[first + u] = piv[u]
    return mats, pivots


def inverse_factors(mats, width):
    sub = lax.broadcasted_iota(jnp.int32, (8, 128), 0)
    lane = lax.broadcasted_iota(jnp.int32, (8, 128), 1)
    tiled = [[m[8 * i : 8 * i + 8, :] for i in range(16)] for m in mats]
    done, pivots = factor(tiled, 128, width)
    inverses = [
        jnp.concatenate(
            [
                jnp.where(lane <= sub + 8 * i, d[i] * lax.rsqrt(p[i]), 0.0)
                for i in range(16)
            ],
            axis=0,
        )
        for d, p in zip(done, pivots)
    ]
    return inverses, pivots


def eye128():
    sub = lax.broadcasted_iota(jnp.int32, (128, 128), 0)
    lane = lax.broadcasted_iota(jnp.int32, (128, 128), 1)
    return jnp.where(sub == lane, 1.0, 0.0)


def eliminate(mats, stacks, width):
    inverses, _ = inverse_factors(mats, width)
    out = []
    for stack, inv in zip(stacks, inverses):
        half = dot_nt(stack, inv)
        out.append(dot_nt(half, half[: half.shape[0] - HROWS]))
    return out


def gather_kernel(
    pat_ref, a_ref, c_ref, r_ref, y_ref, ao_ref, co_ref, ro_ref, xo_ref, x_ref,
    near_s, near_r, far_s, far_r, pass_s, pass_r, own,
):
    me = lax.axis_index("tm")
    slot = lax.rem(me, GROUP)
    base = me - slot
    core = lax.rem(slot, 2)
    far_slot = lax.rem(slot + 2, GROUP)
    near = {"tm": me + 1 - 2 * core}
    far = {"tm": base + far_slot}
    barrier = pltpu.get_barrier_semaphore()
    for peer in (near, far):
        pl.semaphore_signal(barrier, inc=1, device_id=peer, device_id_type=MESH_ID)
    x_ref[...] = jnp.zeros((8, 128), F32)
    x_ref[0:1, :] = y_ref[...]
    keep = jnp.where(me > 0, pat_ref[0, 0], 0).astype(F32)
    x_ref[1:2, :] = jnp.full((1, 128), 1.0, F32) * keep
    pl.semaphore_wait(barrier, 2)
    outs = (ao_ref, co_ref, ro_ref, xo_ref)
    mine = (a_ref.at[0], c_ref.at[0], r_ref.at[0], x_ref)

    def send(src, dst, ss, rs, target):
        copy = pltpu.make_async_remote_copy(
            src_ref=src, dst_ref=dst, send_sem=ss, recv_sem=rs, device_id=target, device_id_type=MESH_ID
        )
        copy.start()
        return copy

    far_copies = [
        send(mine[i], outs[i].at[slot], far_s.at[i], far_r.at[i], far) for i in range(4)
    ]
    near_copies = [
        send(mine[i], outs[i].at[slot], near_s.at[i], near_r.at[i], near) for i in range(4)
    ]
    local = [pltpu.make_async_copy(mine[i], outs[i].at[slot], own.at[i]) for i in range(4)]
    for copy in local:
        copy.start()
    passed = []
    for i in range(4):
        far_copies[i].wait_recv()
        passed.append(
            send(outs[i].at[far_slot], outs[i].at[far_slot], pass_s.at[i], pass_r.at[i], near)
        )
    for copy in local:
        copy.wait()
    for copy in far_copies:
        copy.wait_send()
    for copy in near_copies + passed:
        copy.wait()


def group_gather(pattern, diag_blocks, coupling, arrow_cols, rhs):
    dma = pltpu.SemaphoreType.DMA
    return pl.pallas_call(
        gather_kernel,
        out_shape=(
            VM((GROUP, 128, 128), F32),
            VM((GROUP, 128, 128), F32),
            VM((GROUP, 64, 128), F32),
            VM((GROUP, 8, 128), F32),
        ),
        in_specs=[sspec()] + [vspec()] * 4,
        out_specs=(vspec(),) * 4,
        scratch_shapes=[VM((8, 128), F32)] + [dma((4,))] * 7,
        compiler_params=pltpu.CompilerParams(collective_id=0, has_side_effects=True),
    )(pattern, diag_blocks, coupling, arrow_cols, rhs)


class Blocks:
    def __init__(self, a_ref, c_ref, r_ref, x_ref, shift_ref, couple_ref):
        slot = lax.rem(lax.axis_index("tm"), GROUP)
        self.refs = (a_ref, c_ref, r_ref, x_ref)
        self.shift, self.couple = shift_ref[slot], couple_ref[slot]

    def diag(self, i):
        return self.refs[0][i] + self.shift * eye128()

    def coup(self, i):
        return self.refs[1][i] * (self.refs[3][i, 1:2, :] * self.couple)

    def right(self, i):
        x = self.refs[3][i]
        sub = lax.broadcasted_iota(jnp.int32, (8, 128), 0)
        return jnp.concatenate([self.refs[2][i], jnp.where(sub == 0, x, 0.0)], axis=0)


def local_blocks(blocks, send_state, send_right, d_ref, e_ref, u_ref, h_ref, g_ref):
    diag, coup, right = blocks.diag, blocks.coup, blocks.right
    m0 = jnp.concatenate([coup(1), coup(0), right(0)], axis=0)
    m2 = jnp.concatenate([coup(3), coup(2), right(2)], axis=0)
    ga, gb = eliminate([diag(0), diag(2)], [m0, m2], 8)
    d1 = diag(1) - ga[0:128, 0:128]
    ub = gb[128:256, 128:256]
    (inv_d,), _ = inverse_factors([d1 - ub], 8)
    eb = -gb[0:128, 128:256]
    half_e = dot_nt(eb, inv_d)
    d_ref[2] = diag(3) - gb[0:128, 0:128] - dot_nt(half_e, half_e)
    send_state()
    h1 = right(1) - ga[256:328, 0:128]
    gvb = -gb[256:328, 128:256]
    half_h = dot_nt(h1 + gvb, inv_d)
    h_ref[2] = right(3) - gb[256:328, 0:128] - dot_nt(half_h, half_e)
    send_right()
    u1 = ga[128:256, 128:256]
    et1 = -ga[128:256, 0:128]
    g1 = -ga[256:328, 128:256]
    half_t = dot_nt(et1, inv_d)
    e_ref[2] = -dot_nt(half_e, half_t)
    u_ref[2] = u1 + dot_nt(half_t, half_t)
    g_ref[2] = g1 - dot_nt(half_h, half_t)
    d_ref[0] = d1
    e_ref[0] = -ga[0:128, 128:256]
    u_ref[0] = u1
    h_ref[0] = h1
    g_ref[0] = g1
    (inv_c,), _ = inverse_factors([d1], 8)
    half = dot_nt(jnp.concatenate([coup(2), et1, h1], axis=0), inv_c)
    gc = dot_nt(half, half[0:256])
    d_ref[1] = diag(2) - gc[0:128, 0:128]
    e_ref[1] = -gc[0:128, 128:256]
    u_ref[1] = u1 + gc[128:256, 128:256]
    h_ref[1] = right(2) - gc[256:328, 0:128]
    g_ref[1] = g1 - gc[256:328, 128:256]


def start_copy(src, dst, ss, rs, target):
    copy = pltpu.make_async_remote_copy(
        src_ref=src, dst_ref=dst, send_sem=ss, recv_sem=rs, device_id=target, device_id_type=MESH_ID
    )
    copy.start()
    return copy


def finish_blocks(blocks, sin_ref, win_ref, wait_w, d_ref, e_ref, u_ref, h_ref, g_ref, sum_ref, lf_ref):
    sub = lax.broadcasted_iota(jnp.int32, (8, 128), 0)
    lane = lax.broadcasted_iota(jnp.int32, (8, 128), 1)
    before = sin_ref[...]
    inverses, _ = inverse_factors([before] + [before - u_ref[i] for i in range(3)], 8)
    wait_w()
    w = win_ref[...]
    stacks = [jnp.concatenate([blocks.coup(0), w], axis=0)] + [
        jnp.concatenate([e_ref[i], w + g_ref[i]], axis=0) for i in range(3)
    ]
    diags = [blocks.diag(0)] + [d_ref[i] for i in range(3)]
    rights = [blocks.right(0)] + [h_ref[i] for i in range(3)]
    schur, whole = [], []
    for stack, inv, d, h in zip(stacks, inverses, diags, rights):
        half = dot_nt(stack, inv)
        gram = dot_nt(half, half[0:128])
        schur.append(d - gram[0:128])
        whole.append(h - gram[128:200])
    inverses, pivots = inverse_factors(schur, 8)
    total = None
    for i in range(GROUP):
        x = dot_nt(whole[i], inverses[i])
        gram = dot_nt(x, x)
        total = gram if total is None else total + gram
        logs = jnp.zeros((8, 128), F32)
        for k in range(16):
            logs = logs + jnp.where(lane == sub + 8 * k, pivots[i][k], 0.0)
        lf_ref[i] = jnp.where(
            sub == 0,
            0.5 * jnp.log(jnp.sum(logs, axis=0, keepdims=True)),
            jnp.where(sub == 1, x[64:65, :], 0.0),
        )
    total = jnp.concatenate([total, jnp.zeros((HROWS, 128 - HROWS), F32)], axis=1)
    wide_lane = lax.broadcasted_iota(jnp.int32, (32, 128), 1)
    sum_ref[0:32, :] = jnp.where(wide_lane < 64, total[0:32], pltpu.roll(total[32:64], 64, 1))
    sum_ref[32:40, :] = total[64:72]


def solve_tip(packed, tip_diag, tip_rhs):
    sub = lax.broadcasted_iota(jnp.int32, (8, 128), 0)
    lane = lax.broadcasted_iota(jnp.int32, (8, 128), 1)
    pad = jnp.zeros((1, 64), F32)
    diag = jnp.concatenate([tip_diag, pad], axis=1)
    rhs = jnp.concatenate([tip_rhs, pad], axis=1) - packed[32:33]
    gram = jnp.concatenate([packed[0:32], pltpu.roll(packed[0:32], 64, 1)], axis=0)
    mat = []
    for i in range(8):
        on = lane == sub + 8 * i
        column = jnp.sum(jnp.where(on, rhs, 0.0), axis=1, keepdims=True)
        own = jnp.where(on, diag, 0.0) - gram[8 * i : 8 * i + 8]
        mat.append(jnp.where(lane < 64, own, jnp.where(lane == 64, column, 0.0)))
    (done,), (pivots,) = factor([mat], 64, 8)
    logs = jnp.zeros((8, 128), F32)
    solved = jnp.zeros((8, 128), F32)
    for i in range(8):
        on = lane == sub + 8 * i
        logs = logs + jnp.where(on, jnp.log(pivots[i]), 0.0)
        solved = solved + jnp.where(on, lane_of(done[i], 64) * lax.rsqrt(pivots[i]), 0.0)
    logs = 0.5 * jnp.sum(logs, axis=0, keepdims=True)
    return jnp.where(sub == 0, logs, jnp.sum(solved, axis=0, keepdims=True))


def main_kernel(
    chunks, times, a_ref, c_ref, r_ref, x_ref, shift_ref, couple_ref, tdiag_ref, trhs_ref, lf_in, tip_in,
    d_ref, e_ref, u_ref, h_ref, g_ref, sin_ref, win_ref, s_out, w_out, sum_ref, lf_ref,
    plane_in, acc_in, tip_out, send, recv, acc_s, acc_r,
    lf_s, lf_r, plane_s, plane_r, tip_s, tip_r,
):
    tm, me = lax.axis_index("tm"), lax.axis_index("mesh")
    slot = lax.rem(tm, GROUP)
    seg = tm // GROUP
    segs = times // GROUP
    group = [tm - slot + lax.rem(slot + d, GROUP) for d in range(1, GROUP)]
    plane = [lax.rem(me + d, chunks) for d in range(1, chunks)]
    column = [lax.rem(tm + d, times) for d in range(1, times)]
    later = {"tm": tm + GROUP}
    earlier = {"tm": tm - GROUP}
    barrier = pltpu.get_barrier_semaphore()
    targets = [{"mesh": m} for m in plane] + [{"tm": t} for t in group]
    for target in targets:
        pl.semaphore_signal(barrier, inc=1, device_id=target, device_id_type=MESH_ID)

    @pl.when(seg > 0)
    def _():
        pl.semaphore_signal(barrier, inc=1, device_id=earlier, device_id_type=MESH_ID)

    @pl.when(seg < segs - 1)
    def _():
        pl.semaphore_signal(barrier, inc=1, device_id=later, device_id_type=MESH_ID)

    greeted = len(targets) + (seg > 0).astype(jnp.int32) + (seg < segs - 1).astype(jnp.int32)

    blocks = Blocks(a_ref, c_ref, r_ref, x_ref, shift_ref, couple_ref)
    parts = (d_ref, e_ref, u_ref, h_ref, g_ref)

    def copies(s_src, w_src):
        return [
            pltpu.make_async_remote_copy(
                src_ref=src, dst_ref=dst, send_sem=send.at[i], recv_sem=recv.at[i],
                device_id=later, device_id_type=MESH_ID,
            )
            for i, (src, dst) in enumerate([(s_src, sin_ref), (w_src, win_ref)])
        ]

    def send_state():
        pl.semaphore_wait(barrier, greeted)

        def begin(_, carry):
            copies(d_ref.at[2], h_ref.at[2])[0].start()
            return carry

        lax.fori_loop(0, (seg == 0).astype(jnp.int32), begin, 0)

        @pl.when(seg == 0)
        def _():
            sin_ref[...] = eye128()
            win_ref[...] = jnp.zeros((HROWS, 128), F32)
            acc_in[...] = jnp.zeros((40, 128), F32)

    def send_right():
        @pl.when(seg == 0)
        def _():
            copies(d_ref.at[2], h_ref.at[2])[1].start()

    local_blocks(blocks, send_state, send_right, *parts)

    @pl.when(seg > 0)
    def _():
        out = copies(s_out, w_out)
        out[0].wait_recv()

        @pl.when(seg < segs - 1)
        def _():
            (inverse,), _ = inverse_factors([sin_ref[...] - u_ref[2]], 8)
            half = dot_nt(e_ref[2], inverse)
            s_out[...] = d_ref[2] - dot_nt(half, half)
            out[0].start()
            out[1].wait_recv()
            w_out[...] = h_ref[2] - dot_nt(dot_nt(win_ref[...] + g_ref[2], inverse), half)
            out[1].start()

    def wait_w():
        @pl.when(seg == segs - 1)
        def _():
            copies(s_out, w_out)[1].wait_recv()

    finish_blocks(blocks, sin_ref, win_ref, wait_w, *parts, sum_ref, lf_ref)

    lf = [
        start_copy(lf_ref.at[lax.rem(slot + d + 1, GROUP)], lf_in.at[slot], lf_s.at[d], lf_r.at[d], {"tm": t})
        for d, t in enumerate(group)
    ]
    lf_in[slot] = lf_ref[slot]

    def pass_sum():
        return pltpu.make_async_remote_copy(
            src_ref=sum_ref, dst_ref=acc_in, send_sem=acc_s, recv_sem=acc_r,
            device_id=later, device_id_type=MESH_ID,
        )

    @pl.when(seg > 0)
    def _():
        pass_sum().wait_recv()

    total = sum_ref[...] + acc_in[...]
    sum_ref[...] = total

    @pl.when(seg < segs - 1)
    def _():
        pass_sum().start()

    @pl.when(seg == segs - 1)
    def _():
        share = [
            start_copy(sum_ref, plane_in.at[me], plane_s.at[d], plane_r.at[d], {"mesh": m})
            for d, m in enumerate(plane)
        ]
        plane_in[me] = total
        for copy in share:
            copy.wait_recv()
        whole = plane_in[0]
        for m in range(1, chunks):
            whole = whole + plane_in[m]
        result = solve_tip(whole, tdiag_ref[...], trhs_ref[...])
        tip_out[...] = result
        spread = [
            start_copy(tip_out, tip_in.at[slot], tip_s.at[d], tip_r.at[slot], {"tm": t})
            for d, t in enumerate(column)
        ]
        tip_in[slot] = result
        for copy in share + spread:
            copy.wait_send()

    for copy in lf:
        copy.wait()
    for c in range(GROUP):

        @pl.when(tm != times - GROUP + c)
        def _():
            pltpu.make_async_remote_copy(
                src_ref=tip_out, dst_ref=tip_in.at[c], send_sem=tip_s.at[0], recv_sem=tip_r.at[c],
                device_id=later, device_id_type=MESH_ID,
            ).wait_recv()

    @pl.when(seg < segs - 1)
    def _():
        for copy in copies(s_out, w_out):
            copy.wait_send()
        pass_sum().wait_send()


def main_phase(gathered, config_shift, config_coupling, tip_diag, tip_rhs, chunks, times):
    dma = pltpu.SemaphoreType.DMA
    tile, strip = (128, 128), (HROWS, 128)
    return pl.pallas_call(
        functools.partial(main_kernel, chunks, times),
        out_shape=(VM((GROUP, 8, 128), F32), VM((GROUP, 8, 128), F32)),
        in_specs=[vspec()] * 4 + [sspec()] * 2 + [vspec()] * 2,
        out_specs=(vspec(),) * 2,
        scratch_shapes=[VM((3,) + tile, F32)] * 3
        + [VM((3,) + strip, F32)] * 2
        + [VM(tile, F32), VM(strip, F32)] * 2
        + [
            VM((40, 128), F32),
            VM((GROUP, 8, 128), F32),
            VM((chunks, 40, 128), F32),
            VM((40, 128), F32),
            VM((8, 128), F32),
        ]
        + [dma((2,))] * 2
        + [dma] * 2
        + [dma((GROUP - 1,))] * 2
        + [dma((chunks - 1,))] * 2
        + [dma((times - 1,)), dma((GROUP,))],
        compiler_params=pltpu.CompilerParams(collective_id=1, has_side_effects=True),
    )(*gathered, config_shift, config_coupling, tip_diag[None], tip_rhs[None])


def write_kernel(lf_ref, tip_ref, log_ref, fwd_ref, tlog_ref, tfwd_ref):
    for c in range(GROUP):
        log_ref[c] = lf_ref[c, 0:1, :]
        fwd_ref[c] = lf_ref[c, 1:2, :]
        tlog_ref[c : c + 1, :] = tip_ref[c, 0:1, 0:64]
        tfwd_ref[c : c + 1, :] = tip_ref[c, 1:2, 0:64]


def write_phase(lf, tip):
    wide = jax.ShapeDtypeStruct((GROUP, 1, 128), F32)
    narrow = jax.ShapeDtypeStruct((GROUP, 64), F32)
    return pl.pallas_call(
        write_kernel,
        out_shape=(wide, wide, narrow, narrow),
        in_specs=[vspec()] * 2,
        out_specs=(vspec(),) * 4,
    )(lf, tip)


def shards(
    diag_blocks, coupling, arrow_cols, rhs, tip_rhs, tip_diag, config_shift, config_coupling, pattern
):
    times, chunks = lax.axis_size("tm"), lax.axis_size("mesh")
    gathered = group_gather(pattern, diag_blocks, coupling, arrow_cols, rhs)
    gathered = [pltpu.with_memory_space_constraint(v, pltpu.VMEM) for v in gathered]
    results = main_phase(gathered, config_shift, config_coupling, tip_diag, tip_rhs, chunks, times)
    return write_phase(*[pltpu.with_memory_space_constraint(v, pltpu.VMEM) for v in results])


def solution(mesh):
    in_specs = (
        P("tm", "mesh", None),
        P("tm", "mesh", None),
        P("tm", None, "mesh"),
        P("tm", "mesh"),
        P(),
        P(),
        P(),
        P(),
        P("tm", "mesh"),
    )
    out_specs = (P(None, "tm", "mesh"), P(None, "tm", "mesh"), P(), P())
    return jax.shard_map(shards, mesh=mesh, in_specs=in_specs, out_specs=out_specs, check_vma=False)
```

```python
import functools

import jax
import jax.numpy as jnp
from jax import lax
from jax.experimental import pallas as pl
from jax.experimental.pallas import tpu as pltpu
from jax.sharding import PartitionSpec as P

F32 = jnp.float32
GROUP = 4
HROWS = 72
MESH_ID = pl.DeviceIdType.MESH
VM = pltpu.VMEM
NT = (((1,), (1,)), ((), ()))
NN = (((1,), (0,)), ((), ()))


def vspec():
    return pl.BlockSpec(memory_space=pltpu.VMEM)


def sspec():
    return pl.BlockSpec(memory_space=pltpu.SMEM)


def halves(x):
    high = x.astype(jnp.bfloat16)
    return high, (x - high.astype(F32)).astype(jnp.bfloat16)


def product(a, b, dims):
    ah, al = halves(a)
    bh, bl = halves(b)

    def one(x, y):
        return lax.dot_general(x, y, dims, preferred_element_type=F32)

    return one(ah, bh) + (one(ah, bl) + one(al, bh))


def dot_nt(a, b):
    return product(a, b, NT)


def lane_of(x, j):
    return jnp.broadcast_to(x[:, j : j + 1], x.shape)


def row_of(x, k):
    return jnp.broadcast_to(x[k : k + 1, :], x.shape)


def factor(mats, rows, width):
    tiles, wide = rows // 8, width // 8
    sub = lax.broadcasted_iota(jnp.int32, (8, 128), 0)
    lane = lax.broadcasted_iota(jnp.int32, (8, 128), 1)
    is_row = [sub == k for k in range(8)]
    mats = [list(m) for m in mats]
    pivots = [[None] * tiles for _ in mats]
    for base in range(0, rows, width):
        first = base // 8
        inside = (lane >= base) & (lane < base + width)
        state = []
        for mat in mats:
            panel = [mat[first + u] for u in range(wide)]
            cols = [[lane_of(panel[u], base + j) for u in range(wide)] for j in range(width)]
            panel = [
                jnp.where(inside, jnp.where(lane - base - 8 * u == sub, 1.0, 0.0), panel[u])
                for u in range(wide)
            ]
            ahead = None
            if first + wide < tiles:
                ahead = [
                    [lane_of(mat[first + wide + u], base + j) for j in range(width)]
                    for u in range(wide)
                ]
            state.append((panel, cols, list(panel), [jnp.ones((8, 128), F32)] * wide, ahead))
        for k in range(width):
            tile, row = divmod(k, 8)
            mine = is_row[row]
            for panel, cols, done, piv, _ in state:
                inv = row_of(1.0 / cols[k][tile], row)
                done[tile] = jnp.where(mine, panel[tile], done[tile])
                piv[tile] = jnp.where(mine, cols[k][tile], piv[tile])
                own = list(cols[k])
                own[tile] = jnp.where(mine, own[tile] - 1.0, own[tile])
                own = [part * inv for part in own]
                kept = row_of(panel[tile], row)
                for u in range(wide):
                    panel[u] = panel[u] - own[u] * kept
                for j in range(k + 1, width):
                    kept = row_of(cols[j][tile], row)
                    for u in range(wide):
                        cols[j][u] = cols[j][u] - own[u] * kept
        for (panel, cols, done, piv, ahead), mat, pivs in zip(state, mats, pivots):
            start = first + wide
            if start < tiles:
                spread = [row_of(panel[j // 8], j % 8) for j in range(width)]
                for u in range(wide):
                    terms = [ahead[u][j] * spread[j] for j in range(width)]
                    while len(terms) > 1:
                        terms = [x + y for x, y in zip(terms[::2], terms[1::2])]
                    mat[start + u] = jnp.where(inside, 0.0, mat[start + u]) - terms[0]
                start += wide
            if start < tiles:
                zero = jnp.zeros((8, 128), F32)
                left = jnp.concatenate([jnp.where(inside, mat[q], 0.0) for q in range(start, tiles)], axis=0)
                right = jnp.concatenate([zero] * first + panel + [zero] * (16 - first - wide), axis=0)
                update = product(left, right, NN)
                for q in range(start, tiles):
                    row = 8 * (q - start)
                    mat[q] = jnp.where(inside, 0.0, mat[q]) - update[row : row + 8, :]
            for u in range(wide):
                mat[first + u] = done[u]
                pivs[first + u] = piv[u]
    return mats, pivots


def inverse_factors(mats, width):
    sub = lax.broadcasted_iota(jnp.int32, (8, 128), 0)
    lane = lax.broadcasted_iota(jnp.int32, (8, 128), 1)
    tiled = [[m[8 * i : 8 * i + 8, :] for i in range(16)] for m in mats]
    done, pivots = factor(tiled, 128, width)
    inverses = [
        jnp.concatenate(
            [
                jnp.where(lane <= sub + 8 * i, d[i] * lax.rsqrt(p[i]), 0.0)
                for i in range(16)
            ],
            axis=0,
        )
        for d, p in zip(done, pivots)
    ]
    return inverses, pivots


def eye128():
    sub = lax.broadcasted_iota(jnp.int32, (128, 128), 0)
    lane = lax.broadcasted_iota(jnp.int32, (128, 128), 1)
    return jnp.where(sub == lane, 1.0, 0.0)


def eliminate(mats, stacks, width):
    inverses, _ = inverse_factors(mats, width)
    out = []
    for stack, inv in zip(stacks, inverses):
        half = dot_nt(stack, inv)
        out.append(dot_nt(half, half[: half.shape[0] - HROWS]))
    return out


def gather_kernel(
    pat_ref, a_ref, c_ref, r_ref, y_ref, ao_ref, co_ref, ro_ref, xo_ref, x_ref,
    near_s, near_r, far_s, far_r, pass_s, pass_r, own,
):
    me = lax.axis_index("tm")
    slot = lax.rem(me, GROUP)
    base = me - slot
    core = lax.rem(slot, 2)
    far_slot = lax.rem(slot + 2, GROUP)
    near = {"tm": me + 1 - 2 * core}
    far = {"tm": base + far_slot}
    barrier = pltpu.get_barrier_semaphore()
    for peer in (near, far):
        pl.semaphore_signal(barrier, inc=1, device_id=peer, device_id_type=MESH_ID)
    x_ref[...] = jnp.zeros((8, 128), F32)
    x_ref[0:1, :] = y_ref[...]
    keep = jnp.where(me > 0, pat_ref[0, 0], 0).astype(F32)
    x_ref[1:2, :] = jnp.full((1, 128), 1.0, F32) * keep
    pl.semaphore_wait(barrier, 2)
    outs = (ao_ref, co_ref, ro_ref, xo_ref)
    mine = (a_ref.at[0], c_ref.at[0], r_ref.at[0], x_ref)

    def send(src, dst, ss, rs, target):
        copy = pltpu.make_async_remote_copy(
            src_ref=src, dst_ref=dst, send_sem=ss, recv_sem=rs, device_id=target, device_id_type=MESH_ID
        )
        copy.start()
        return copy

    far_copies = [
        send(mine[i], outs[i].at[slot], far_s.at[i], far_r.at[i], far) for i in range(4)
    ]
    near_copies = [
        send(mine[i], outs[i].at[slot], near_s.at[i], near_r.at[i], near) for i in range(4)
    ]
    local = [pltpu.make_async_copy(mine[i], outs[i].at[slot], own.at[i]) for i in range(4)]
    for copy in local:
        copy.start()
    passed = []
    for i in range(4):
        far_copies[i].wait_recv()
        passed.append(
            send(outs[i].at[far_slot], outs[i].at[far_slot], pass_s.at[i], pass_r.at[i], near)
        )
    for copy in local:
        copy.wait()
    for copy in far_copies:
        copy.wait_send()
    for copy in near_copies + passed:
        copy.wait()


def group_gather(pattern, diag_blocks, coupling, arrow_cols, rhs):
    dma = pltpu.SemaphoreType.DMA
    return pl.pallas_call(
        gather_kernel,
        out_shape=(
            VM((GROUP, 128, 128), F32),
            VM((GROUP, 128, 128), F32),
            VM((GROUP, 64, 128), F32),
            VM((GROUP, 8, 128), F32),
        ),
        in_specs=[sspec()] + [vspec()] * 4,
        out_specs=(vspec(),) * 4,
        scratch_shapes=[VM((8, 128), F32)] + [dma((4,))] * 7,
        compiler_params=pltpu.CompilerParams(collective_id=0, has_side_effects=True),
    )(pattern, diag_blocks, coupling, arrow_cols, rhs)


class Blocks:
    def __init__(self, a_ref, c_ref, r_ref, x_ref, shift_ref, couple_ref):
        slot = lax.rem(lax.axis_index("tm"), GROUP)
        self.refs = (a_ref, c_ref, r_ref, x_ref)
        self.shift, self.couple = shift_ref[slot], couple_ref[slot]

    def diag(self, i):
        return self.refs[0][i] + self.shift * eye128()

    def coup(self, i):
        return self.refs[1][i] * (self.refs[3][i, 1:2, :] * self.couple)

    def right(self, i):
        x = self.refs[3][i]
        sub = lax.broadcasted_iota(jnp.int32, (8, 128), 0)
        return jnp.concatenate([self.refs[2][i], jnp.where(sub == 0, x, 0.0)], axis=0)


def local_blocks(blocks, send_state, send_right, d_ref, e_ref, u_ref, h_ref, g_ref):
    diag, coup, right = blocks.diag, blocks.coup, blocks.right
    m0 = jnp.concatenate([coup(1), coup(0), right(0)], axis=0)
    m2 = jnp.concatenate([coup(3), coup(2), right(2)], axis=0)
    ga, gb = eliminate([diag(0), diag(2)], [m0, m2], 8)
    d1 = diag(1) - ga[0:128, 0:128]
    ub = gb[128:256, 128:256]
    (inv_c, inv_d), _ = inverse_factors([d1, d1 - ub], 8)
    eb = -gb[0:128, 128:256]
    half_e = dot_nt(eb, inv_d)
    d_ref[2] = diag(3) - gb[0:128, 0:128] - dot_nt(half_e, half_e)
    send_state()
    h1 = right(1) - ga[256:328, 0:128]
    gvb = -gb[256:328, 128:256]
    half_h = dot_nt(h1 + gvb, inv_d)
    h_ref[2] = right(3) - gb[256:328, 0:128] - dot_nt(half_h, half_e)
    send_right()
    u1 = ga[128:256, 128:256]
    et1 = -ga[128:256, 0:128]
    g1 = -ga[256:328, 128:256]
    half_t = dot_nt(et1, inv_d)
    e_ref[2] = -dot_nt(half_e, half_t)
    u_ref[2] = u1 + dot_nt(half_t, half_t)
    g_ref[2] = g1 - dot_nt(half_h, half_t)
    d_ref[0] = d1
    e_ref[0] = -ga[0:128, 128:256]
    u_ref[0] = u1
    h_ref[0] = h1
    g_ref[0] = g1
    half = dot_nt(jnp.concatenate([coup(2), et1, h1], axis=0), inv_c)
    gc = dot_nt(half, half[0:256])
    d_ref[1] = diag(2) - gc[0:128, 0:128]
    e_ref[1] = -gc[0:128, 128:256]
    u_ref[1] = u1 + gc[128:256, 128:256]
    h_ref[1] = right(2) - gc[256:328, 0:128]
    g_ref[1] = g1 - gc[256:328, 128:256]


def start_copy(src, dst, ss, rs, target):
    copy = pltpu.make_async_remote_copy(
        src_ref=src, dst_ref=dst, send_sem=ss, recv_sem=rs, device_id=target, device_id_type=MESH_ID
    )
    copy.start()
    return copy


def finish_blocks(blocks, sin_ref, win_ref, wait_w, d_ref, e_ref, u_ref, h_ref, g_ref, sum_ref, lf_ref):
    sub = lax.broadcasted_iota(jnp.int32, (8, 128), 0)
    lane = lax.broadcasted_iota(jnp.int32, (8, 128), 1)
    before = sin_ref[...]
    inverses, _ = inverse_factors([before] + [before - u_ref[i] for i in range(3)], 8)
    wait_w()
    w = win_ref[...]
    stacks = [jnp.concatenate([blocks.coup(0), w], axis=0)] + [
        jnp.concatenate([e_ref[i], w + g_ref[i]], axis=0) for i in range(3)
    ]
    diags = [blocks.diag(0)] + [d_ref[i] for i in range(3)]
    rights = [blocks.right(0)] + [h_ref[i] for i in range(3)]
    schur, whole = [], []
    for stack, inv, d, h in zip(stacks, inverses, diags, rights):
        half = dot_nt(stack, inv)
        gram = dot_nt(half, half[0:128])
        schur.append(d - gram[0:128])
        whole.append(h - gram[128:200])
    inverses, pivots = inverse_factors(schur, 8)
    total = None
    for i in range(GROUP):
        x = dot_nt(whole[i], inverses[i])
        gram = dot_nt(x, x)
        total = gram if total is None else total + gram
        logs = jnp.zeros((8, 128), F32)
        for k in range(16):
            logs = logs + jnp.where(lane == sub + 8 * k, pivots[i][k], 0.0)
        lf_ref[i] = jnp.where(
            sub == 0,
            0.5 * jnp.log(jnp.sum(logs, axis=0, keepdims=True)),
            jnp.where(sub == 1, x[64:65, :], 0.0),
        )
    total = jnp.concatenate([total, jnp.zeros((HROWS, 128 - HROWS), F32)], axis=1)
    wide_lane = lax.broadcasted_iota(jnp.int32, (32, 128), 1)
    sum_ref[0:32, :] = jnp.where(wide_lane < 64, total[0:32], pltpu.roll(total[32:64], 64, 1))
    sum_ref[32:40, :] = total[64:72]


def solve_tip(packed, tip_diag, tip_rhs):
    sub = lax.broadcasted_iota(jnp.int32, (8, 128), 0)
    lane = lax.broadcasted_iota(jnp.int32, (8, 128), 1)
    pad = jnp.zeros((1, 64), F32)
    diag = jnp.concatenate([tip_diag, pad], axis=1)
    rhs = jnp.concatenate([tip_rhs, pad], axis=1) - packed[32:33]
    gram = jnp.concatenate([packed[0:32], pltpu.roll(packed[0:32], 64, 1)], axis=0)
    mat = []
    for i in range(8):
        on = lane == sub + 8 * i
        column = jnp.sum(jnp.where(on, rhs, 0.0), axis=1, keepdims=True)
        own = jnp.where(on, diag, 0.0) - gram[8 * i : 8 * i + 8]
        mat.append(jnp.where(lane < 64, own, jnp.where(lane == 64, column, 0.0)))
    (done,), (pivots,) = factor([mat], 64, 16)
    logs = jnp.zeros((8, 128), F32)
    solved = jnp.zeros((8, 128), F32)
    for i in range(8):
        on = lane == sub + 8 * i
        logs = logs + jnp.where(on, jnp.log(pivots[i]), 0.0)
        solved = solved + jnp.where(on, lane_of(done[i], 64) * lax.rsqrt(pivots[i]), 0.0)
    logs = 0.5 * jnp.sum(logs, axis=0, keepdims=True)
    return jnp.where(sub == 0, logs, jnp.sum(solved, axis=0, keepdims=True))


def main_kernel(
    chunks, times, a_ref, c_ref, r_ref, x_ref, shift_ref, couple_ref, tdiag_ref, trhs_ref, lf_in, tip_in,
    d_ref, e_ref, u_ref, h_ref, g_ref, sin_ref, win_ref, s_out, w_out, sum_ref, lf_ref,
    plane_in, acc_in, tip_out, send, recv, acc_s, acc_r,
    lf_s, lf_r, plane_s, plane_r, tip_s, tip_r,
):
    tm, me = lax.axis_index("tm"), lax.axis_index("mesh")
    slot = lax.rem(tm, GROUP)
    seg = tm // GROUP
    segs = times // GROUP
    group = [tm - slot + lax.rem(slot + d, GROUP) for d in range(1, GROUP)]
    plane = [lax.rem(me + d, chunks) for d in range(1, chunks)]
    column = [lax.rem(tm + d, times) for d in range(1, times)]
    later = {"tm": tm + GROUP}
    earlier = {"tm": tm - GROUP}
    barrier = pltpu.get_barrier_semaphore()
    targets = [{"mesh": m} for m in plane] + [{"tm": t} for t in group]
    for target in targets:
        pl.semaphore_signal(barrier, inc=1, device_id=target, device_id_type=MESH_ID)

    @pl.when(seg > 0)
    def _():
        pl.semaphore_signal(barrier, inc=1, device_id=earlier, device_id_type=MESH_ID)

    @pl.when(seg < segs - 1)
    def _():
        pl.semaphore_signal(barrier, inc=1, device_id=later, device_id_type=MESH_ID)

    greeted = len(targets) + (seg > 0).astype(jnp.int32) + (seg < segs - 1).astype(jnp.int32)

    blocks = Blocks(a_ref, c_ref, r_ref, x_ref, shift_ref, couple_ref)
    parts = (d_ref, e_ref, u_ref, h_ref, g_ref)

    def copies(s_src, w_src):
        return [
            pltpu.make_async_remote_copy(
                src_ref=src, dst_ref=dst, send_sem=send.at[i], recv_sem=recv.at[i],
                device_id=later, device_id_type=MESH_ID,
            )
            for i, (src, dst) in enumerate([(s_src, sin_ref), (w_src, win_ref)])
        ]

    def send_state():
        pl.semaphore_wait(barrier, greeted)

        def begin(_, carry):
            copies(d_ref.at[2], h_ref.at[2])[0].start()
            return carry

        lax.fori_loop(0, (seg == 0).astype(jnp.int32), begin, 0)

        @pl.when(seg == 0)
        def _():
            sin_ref[...] = eye128()
            win_ref[...] = jnp.zeros((HROWS, 128), F32)
            acc_in[...] = jnp.zeros((40, 128), F32)

    def send_right():
        @pl.when(seg == 0)
        def _():
            copies(d_ref.at[2], h_ref.at[2])[1].start()

    local_blocks(blocks, send_state, send_right, *parts)

    @pl.when(seg > 0)
    def _():
        out = copies(s_out, w_out)
        out[0].wait_recv()

        @pl.when(seg < segs - 1)
        def _():
            (inverse,), _ = inverse_factors([sin_ref[...] - u_ref[2]], 16)
            half = dot_nt(e_ref[2], inverse)
            s_out[...] = d_ref[2] - dot_nt(half, half)
            out[0].start()
            out[1].wait_recv()
            w_out[...] = h_ref[2] - dot_nt(dot_nt(win_ref[...] + g_ref[2], inverse), half)
            out[1].start()

    def wait_w():
        @pl.when(seg == segs - 1)
        def _():
            copies(s_out, w_out)[1].wait_recv()

    finish_blocks(blocks, sin_ref, win_ref, wait_w, *parts, sum_ref, lf_ref)

    lf = [
        start_copy(lf_ref.at[lax.rem(slot + d + 1, GROUP)], lf_in.at[slot], lf_s.at[d], lf_r.at[d], {"tm": t})
        for d, t in enumerate(group)
    ]
    lf_in[slot] = lf_ref[slot]

    def pass_sum():
        return pltpu.make_async_remote_copy(
            src_ref=sum_ref, dst_ref=acc_in, send_sem=acc_s, recv_sem=acc_r,
            device_id=later, device_id_type=MESH_ID,
        )

    @pl.when(seg > 0)
    def _():
        pass_sum().wait_recv()

    total = sum_ref[...] + acc_in[...]
    sum_ref[...] = total

    @pl.when(seg < segs - 1)
    def _():
        pass_sum().start()

    @pl.when(seg == segs - 1)
    def _():
        share = [
            start_copy(sum_ref, plane_in.at[me], plane_s.at[d], plane_r.at[d], {"mesh": m})
            for d, m in enumerate(plane)
        ]
        plane_in[me] = total
        for copy in share:
            copy.wait_recv()
        whole = plane_in[0]
        for m in range(1, chunks):
            whole = whole + plane_in[m]
        result = solve_tip(whole, tdiag_ref[...], trhs_ref[...])
        tip_out[...] = result
        spread = [
            start_copy(tip_out, tip_in.at[slot], tip_s.at[d], tip_r.at[slot], {"tm": t})
            for d, t in enumerate(column)
        ]
        tip_in[slot] = result
        for copy in share + spread:
            copy.wait_send()

    for copy in lf:
        copy.wait()
    for c in range(GROUP):

        @pl.when(tm != times - GROUP + c)
        def _():
            pltpu.make_async_remote_copy(
                src_ref=tip_out, dst_ref=tip_in.at[c], send_sem=tip_s.at[0], recv_sem=tip_r.at[c],
                device_id=later, device_id_type=MESH_ID,
            ).wait_recv()

    @pl.when(seg < segs - 1)
    def _():
        for copy in copies(s_out, w_out):
            copy.wait_send()
        pass_sum().wait_send()


def main_phase(gathered, config_shift, config_coupling, tip_diag, tip_rhs, chunks, times):
    dma = pltpu.SemaphoreType.DMA
    tile, strip = (128, 128), (HROWS, 128)
    return pl.pallas_call(
        functools.partial(main_kernel, chunks, times),
        out_shape=(VM((GROUP, 8, 128), F32), VM((GROUP, 8, 128), F32)),
        in_specs=[vspec()] * 4 + [sspec()] * 2 + [vspec()] * 2,
        out_specs=(vspec(),) * 2,
        scratch_shapes=[VM((3,) + tile, F32)] * 3
        + [VM((3,) + strip, F32)] * 2
        + [VM(tile, F32), VM(strip, F32)] * 2
        + [
            VM((40, 128), F32),
            VM((GROUP, 8, 128), F32),
            VM((chunks, 40, 128), F32),
            VM((40, 128), F32),
            VM((8, 128), F32),
        ]
        + [dma((2,))] * 2
        + [dma] * 2
        + [dma((GROUP - 1,))] * 2
        + [dma((chunks - 1,))] * 2
        + [dma((times - 1,)), dma((GROUP,))],
        compiler_params=pltpu.CompilerParams(collective_id=1, has_side_effects=True),
    )(*gathered, config_shift, config_coupling, tip_diag[None], tip_rhs[None])


def write_kernel(lf_ref, tip_ref, log_ref, fwd_ref, tlog_ref, tfwd_ref):
    for c in range(GROUP):
        log_ref[c] = lf_ref[c, 0:1, :]
        fwd_ref[c] = lf_ref[c, 1:2, :]
        tlog_ref[c : c + 1, :] = tip_ref[c, 0:1, 0:64]
        tfwd_ref[c : c + 1, :] = tip_ref[c, 1:2, 0:64]


def write_phase(lf, tip):
    wide = jax.ShapeDtypeStruct((GROUP, 1, 128), F32)
    narrow = jax.ShapeDtypeStruct((GROUP, 64), F32)
    return pl.pallas_call(
        write_kernel,
        out_shape=(wide, wide, narrow, narrow),
        in_specs=[vspec()] * 2,
        out_specs=(vspec(),) * 4,
    )(lf, tip)


def shards(
    diag_blocks, coupling, arrow_cols, rhs, tip_rhs, tip_diag, config_shift, config_coupling, pattern
):
    times, chunks = lax.axis_size("tm"), lax.axis_size("mesh")
    gathered = group_gather(pattern, diag_blocks, coupling, arrow_cols, rhs)
    gathered = [pltpu.with_memory_space_constraint(v, pltpu.VMEM) for v in gathered]
    results = main_phase(gathered, config_shift, config_coupling, tip_diag, tip_rhs, chunks, times)
    return write_phase(*[pltpu.with_memory_space_constraint(v, pltpu.VMEM) for v in results])


def solution(mesh):
    in_specs = (
        P("tm", "mesh", None),
        P("tm", "mesh", None),
        P("tm", None, "mesh"),
        P("tm", "mesh"),
        P(),
        P(),
        P(),
        P(),
        P("tm", "mesh"),
    )
    out_specs = (P(None, "tm", "mesh"), P(None, "tm", "mesh"), P(), P())
    return jax.shard_map(shards, mesh=mesh, in_specs=in_specs, out_specs=out_specs, check_vma=False)
```
